32 devices in a mesh: dom: 8 (over y, x, core), group: 4 (over z).
Axes of the slice: x: 2, y: 2, z: 4, core: 2. Of those that a mesh axis runs over, the one named last changes fastest.
Arguments:
- nodes: bfloat16 [32, 256, 128], P(('dom', 'group')), may hold values from -6 to 6
- edges: bfloat16 [32, 1536, 128], P(('dom', 'group')), may hold values from -6 to 6
- node_cot: bfloat16 [32, 256, 128], P(('dom', 'group')), may hold values from -6 to 6
- send_index: int32 [32, 4, 128], P(('dom', 'group')), may hold values from 0 to 255
- halo_count: int32 [32, 4], P(('dom', 'group')), may hold values from 0 to 128, as said below
- senders: int32 [32, 1536], P(('dom', 'group')), may hold values from 0 to 767, as said below
- receivers: int32 [32, 1536], P(('dom', 'group')), may hold values from 0 to 255, as said below
- edge_in_w: bfloat16 [2, 384, 128], replicated, may hold values from -0.3125 to 0.3125
- edge_out_w: bfloat16 [2, 128, 128], replicated, may hold values from -0.5 to 0.5
- node_in_w: bfloat16 [2, 256, 128], replicated, may hold values from -0.375 to 0.375
- node_out_w: bfloat16 [2, 128, 128], replicated, may hold values from -0.5 to 0.5
- biases: float32 [2, 4, 128], replicated, may hold values from -3 to 3
- gains: float32 [2, 2, 128], replicated, may hold values from 0.1 to 1.9
Outputs:
- nodes_out: bfloat16 [32, 256, 128], P(('dom', 'group'))
- node_grad: bfloat16 [32, 256, 128], P(('dom', 'group'))
- edge_grad: bfloat16 [32, 1536, 128], P(('dom', 'group'))
- edge_in_grad: float32 [2, 384, 128], replicated
- edge_out_grad: float32 [2, 128, 128], replicated
- node_in_grad: float32 [2, 256, 128], replicated
- node_out_grad: float32 [2, 128, 128], replicated
- bias_grad: float32 [2, 4, 128], replicated
- gain_grad: float32 [2, 2, 128], replicated
The draws below stay inside these ranges and needn't reach their ends.
Inputs may be any that keep to these rules, and one draw needn't show every extreme that they name: `halo_count`: slot order: from the lower then the upper partition along dom, then along group; 0 exactly where that neighbour does not exist; every slot reaches 128 on some partition. `senders`: below 256: a node of the partition; 256 + s: the s-th live halo row of the table, s below the partition's total halo_count. `receivers`: never fall along a partition's edges; within each aligned block of 512 edges they span fewer than 128 nodes.
All inputs are finite; a program needn't handle non-finite values.
Results may differ from the reference program's by a relative error of at most 0.02.
Values may be sent and summed in bfloat16 or wider, within the bound.
A program may use at most 64 MiB of HBM per device.

```python
from functools import partial
import jax
import jax.numpy as jnp
from jax import lax

H = 128
L = 2
NODE_DEV = 256
HALO = 128
EDGE_DEV = 1536
PARTITIONS = 32
N_DOM = 8
N_GROUP = 4


def counts_table(key):
    base_key = jax.random.fold_in(key, 7)
    first_key, second_key = jax.random.split(base_key)
    partition = jnp.arange(PARTITIONS, dtype=jnp.int32)
    dom_place = partition // N_GROUP
    group_place = partition % N_GROUP
    present = jnp.stack([dom_place > 0, dom_place < N_DOM - 1, group_place > 0, group_place < N_GROUP - 1], axis=1)
    drawn = jax.random.randint(first_key, (PARTITIONS, 4), HALO // 4, HALO + 1)
    scores = jnp.where(present, jax.random.randint(second_key, (PARTITIONS, 4), 0, 1 << 30), -1)
    topmost = scores == jnp.max(scores, axis=0, keepdims=True)
    drawn = jnp.where(topmost, HALO, drawn)
    drawn = jnp.where((partition == N_GROUP + 1)[:, None], HALO, drawn)
    return jnp.where(present, drawn, 0).astype(jnp.int32)


def draw_halo_count(key, part):
    return counts_table(key)


def draw_senders(key, part):
    counts = counts_table(key)
    live_rows = jnp.sum(counts, axis=1).astype(jnp.int32)
    base_key = jax.random.fold_in(key, 11)
    local_key, pick_key, mode_key = jax.random.split(base_key, 3)
    local_ids = jax.random.randint(local_key, (PARTITIONS, EDGE_DEV), 0, NODE_DEV)
    picks = jax.random.randint(pick_key, (PARTITIONS, EDGE_DEV), 0, 1 << 30)
    remote_ids = NODE_DEV + picks % live_rows[:, None]
    choose_remote = jax.random.randint(mode_key, (PARTITIONS, EDGE_DEV), 0, 4) == 0
    chosen = jnp.where(choose_remote, remote_ids, local_ids).astype(jnp.int32)
    last_live = (NODE_DEV + live_rows - 1).astype(jnp.int32)
    first_edge = jnp.arange(EDGE_DEV, dtype=jnp.int32) == 0
    return jnp.where(first_edge[None, :], last_live[:, None], chosen).astype(jnp.int32)


def draw_receivers(key, part):
    base_key = jax.random.fold_in(key, 23)
    ramp_rows = jnp.arange(EDGE_DEV, dtype=jnp.int32) * NODE_DEV // EDGE_DEV
    jitter = jax.random.randint(base_key, (PARTITIONS, EDGE_DEV), 0, 32)
    return jnp.clip(jnp.sort(ramp_rows[None, :] + jitter, axis=1), 0, NODE_DEV - 1).astype(jnp.int32)


def touch_ends(array, key, least, top_value):
    index_at = [jax.random.randint(jax.random.fold_in(key, axis), (), 0, length) for axis, length in enumerate(array.shape)]
    main_axis = array.shape.index(max(array.shape))
    neighbour = index_at[:main_axis] + [(index_at[main_axis] + 1) % array.shape[main_axis]] + index_at[main_axis + 1:]
    return array.at[tuple(index_at)].set(least).at[tuple(neighbour)].set(top_value)


def levels(rng, dims, pieces, smallest, largest):
    gain, own = 1.0, jax.random.fold_in(rng, 6)
    for position, blocks in pieces:
        steps = jnp.exp(jax.random.uniform(jax.random.fold_in(own, position), (blocks,), jnp.float32, smallest / len(pieces), largest / len(pieces)))
        gain = gain * jnp.repeat(steps, dims[position] // blocks).reshape([-1 if axis == position else 1 for axis in range(len(dims))])
    return gain


def normal_values(rng, shape, width, most, shards=(), kind=jnp.bfloat16):
    gain = levels(rng, shape, shards, -0.22, 0.18) if shards else 1.0
    entries = jax.random.normal(rng, shape, jnp.float32) * width * gain
    return jnp.minimum(jnp.maximum(entries, -most), most).astype(kind)


def setup_inputs(seed: int = 0) -> dict:
    seeds = jax.random.split(jax.random.key(seed), 14)
    nodes = normal_values(seeds[0], (PARTITIONS, NODE_DEV, H), 1.0, 6.0, ((0, 32),))
    edges = normal_values(seeds[1], (PARTITIONS, EDGE_DEV, H), 1.0, 6.0, ((0, 32),))
    node_cot = normal_values(seeds[2], (PARTITIONS, NODE_DEV, H), 1.0, 6.0, ((0, 32),))
    send_index = touch_ends(jax.random.randint(seeds[3], (PARTITIONS, 4, HALO), 0, NODE_DEV), jax.random.fold_in(seeds[3], 1), 0, NODE_DEV - 1).astype(jnp.int32)
    halo_count = draw_halo_count(jax.random.fold_in(seeds[13], 71), 0)
    senders = draw_senders(jax.random.fold_in(seeds[13], 71), 0)
    receivers = draw_receivers(jax.random.fold_in(seeds[13], 71), 0)
    edge_in_w = normal_values(seeds[7], (L, 3 * H, H), (3 * H) ** -0.5, 0.3125)
    edge_out_w = normal_values(seeds[8], (L, H, H), H ** -0.5, 0.5)
    node_in_w = normal_values(seeds[9], (L, 2 * H, H), (2 * H) ** -0.5, 0.375)
    node_out_w = normal_values(seeds[10], (L, H, H), H ** -0.5, 0.5)
    biases = normal_values(seeds[11], (L, 4, H), 0.5, 3.0, (), jnp.float32)
    gains = jnp.clip(1.0 + 0.18 * jax.random.normal(seeds[12], (L, 2, H), jnp.float32), 0.1, 1.9)
    return dict(nodes=nodes, edges=edges, node_cot=node_cot, send_index=send_index, halo_count=halo_count, senders=senders, receivers=receivers, edge_in_w=edge_in_w, edge_out_w=edge_out_w, node_in_w=node_in_w, node_out_w=node_out_w, biases=biases, gains=gains)


def norm_rows(values, gain_row):
    centre = values - lax.optimization_barrier(jnp.mean(values, axis=-1, keepdims=True))
    spread = lax.optimization_barrier(jnp.mean(centre * centre, axis=-1, keepdims=True))
    return centre * lax.rsqrt(spread + 1e-05) * gain_row

def pack_halo(received, counts):
    halo_depth = received.shape[1]
    feat_width = received.shape[2]
    block_ends = jnp.cumsum(counts).astype(jnp.int32)
    block_starts = (block_ends - counts).astype(jnp.int32)
    positions = jnp.arange(4 * halo_depth, dtype=jnp.int32)
    block_of = lax.optimization_barrier(jnp.sum((positions[:, None] >= block_ends[None, :]).astype(jnp.int32), axis=1)).astype(jnp.int32)
    clamped = jnp.minimum(block_of, 3)
    selector = jnp.arange(4, dtype=jnp.int32)
    offsets = lax.optimization_barrier(jnp.sum(jnp.where(clamped[:, None] == selector[None, :], block_starts[None, :], 0), axis=1)).astype(jnp.int32)
    within_block = positions - offsets
    sources = clamped * halo_depth + jnp.clip(within_block, 0, halo_depth - 1)
    picked = received.reshape(4 * halo_depth, feat_width)[sources]
    return jnp.where((block_of < 4)[:, None], picked, jnp.zeros_like(picked))

def edge_update(weights, edge_rows, sent_feat, recv_feat):
    edge_in, edge_out, node_in, node_out, bias_rows, gain_rows = weights
    joined = jnp.concatenate([edge_rows, sent_feat, recv_feat], axis=1)
    hidden = jax.nn.silu(jnp.dot(joined, edge_in, preferred_element_type=jnp.float32) + bias_rows[0]).astype(jnp.bfloat16)
    mapped = jnp.dot(hidden, edge_out, preferred_element_type=jnp.float32) + bias_rows[1]
    return (edge_rows.astype(jnp.float32) + norm_rows(mapped, gain_rows[0])).astype(jnp.bfloat16)

def node_update(weights, node_vals, summed):
    edge_in, edge_out, node_in, node_out, bias_rows, gain_rows = weights
    joined = jnp.concatenate([node_vals.astype(jnp.bfloat16), summed.astype(jnp.bfloat16)], axis=1)
    hidden = jax.nn.silu(jnp.dot(joined, node_in, preferred_element_type=jnp.float32) + bias_rows[2]).astype(jnp.bfloat16)
    mapped = jnp.dot(hidden, node_out, preferred_element_type=jnp.float32) + bias_rows[3]
    return (node_vals + norm_rows(mapped, gain_rows[1])).astype(jnp.bfloat16)

def local_layer(weights, edge_rows, node_vals, received, counts, sender_ids, receiver_ids):
    table = jnp.concatenate([node_vals, pack_halo(received, counts)], axis=0)
    sent_feat = table[sender_ids].astype(jnp.bfloat16)
    recv_feat = table[receiver_ids].astype(jnp.bfloat16)
    edge_new = edge_update(weights, edge_rows, sent_feat, recv_feat)
    summed = jax.ops.segment_sum(edge_new.astype(jnp.float32), receiver_ids, num_segments=node_vals.shape[0])
    return (edge_new, node_update(weights, node_vals, summed))

def gather_rows(node_rows, send_rows):
    return node_rows.astype(jnp.float32)[send_rows]

def exchange_rows(node_all, send_index):
    sent_rows = jax.vmap(gather_rows)(node_all, send_index)
    grid_rows = sent_rows.reshape((N_DOM, N_GROUP) + sent_rows.shape[1:])
    zero_dom = jnp.zeros_like(grid_rows[:1, :, 0])
    zero_grp = jnp.zeros_like(grid_rows[:, :1, 0])
    slot_zero = jnp.concatenate([zero_dom, grid_rows[:-1, :, 0]], axis=0)
    slot_one = jnp.concatenate([grid_rows[1:, :, 1], zero_dom], axis=0)
    slot_two = jnp.concatenate([zero_grp, grid_rows[:, :-1, 2]], axis=1)
    slot_three = jnp.concatenate([grid_rows[:, 1:, 3], zero_grp], axis=1)
    return jnp.stack([slot_zero, slot_one, slot_two, slot_three], axis=2).reshape(sent_rows.shape)

def add_rows(returned, send_rows, node_count):
    return jax.ops.segment_sum(returned.reshape(-1, returned.shape[-1]), send_rows.reshape(-1), num_segments=node_count)

def scatter_back(cot_all, send_index, node_count):
    grid_rows = cot_all.reshape((N_DOM, N_GROUP) + cot_all.shape[1:])
    zero_dom = jnp.zeros_like(grid_rows[:1, :, 0])
    zero_grp = jnp.zeros_like(grid_rows[:, :1, 0])
    back_zero = jnp.concatenate([grid_rows[1:, :, 0], zero_dom], axis=0)
    back_one = jnp.concatenate([zero_dom, grid_rows[:-1, :, 1]], axis=0)
    back_two = jnp.concatenate([grid_rows[:, 1:, 2], zero_grp], axis=1)
    back_three = jnp.concatenate([zero_grp, grid_rows[:, :-1, 3]], axis=1)
    returned = jnp.stack([back_zero, back_one, back_two, back_three], axis=2).reshape(cot_all.shape)
    return jax.vmap(partial(add_rows, node_count=node_count))(returned, send_index)

def reference(nodes, edges, node_cot, send_index, halo_count, senders, receivers, edge_in_w, edge_out_w, node_in_w, node_out_w, biases, gains):
    layer_count = edge_in_w.shape[0]
    node_count = nodes.shape[1]
    node_all = nodes
    edge_all = edges
    saved_inputs = []
    for layer_index in range(layer_count):
        weights = (edge_in_w[layer_index], edge_out_w[layer_index], node_in_w[layer_index], node_out_w[layer_index], biases[layer_index], gains[layer_index])
        received = exchange_rows(node_all, send_index)
        saved_inputs.append((edge_all, node_all, received))

        def forward_one(carried, members, weights=weights):
            edge_vals, node_vals, halo_vals, counts, sender_ids, receiver_ids = members
            return (carried, local_layer(weights, edge_vals, node_vals.astype(jnp.float32), halo_vals, counts, sender_ids, receiver_ids))
        unused, (edge_all, node_all) = lax.scan(forward_one, jnp.zeros((), jnp.int32), (edge_all, node_all, received, halo_count, senders, receivers))
    node_cot_all = node_cot
    edge_cot_all = jnp.zeros_like(edges)
    layer_grads = [None] * layer_count
    for layer_index in reversed(range(layer_count)):
        weights = (edge_in_w[layer_index], edge_out_w[layer_index], node_in_w[layer_index], node_out_w[layer_index], biases[layer_index], gains[layer_index])
        edge_in_all, node_in_all, received = saved_inputs[layer_index]

        def backward_one(totals, members, weights=weights):
            edge_vals, node_vals, halo_vals, counts, sender_ids, receiver_ids, edge_cot, node_cot_rows = members

            def layer_call(params, edge_arg, node_arg, halo_arg):
                return local_layer(params, edge_arg, node_arg, halo_arg, counts, sender_ids, receiver_ids)
            outputs, pullback = jax.vjp(layer_call, weights, edge_vals, node_vals.astype(jnp.float32), halo_vals)
            weight_cot, edge_back, node_back, halo_back = pullback((edge_cot, node_cot_rows))
            totals = tuple((running + leaf_val.astype(jnp.float32) for running, leaf_val in zip(totals, weight_cot)))
            return (totals, (edge_back, node_back, halo_back))
        initial = tuple((jnp.zeros(leaf_val.shape, jnp.float32) for leaf_val in weights))
        totals, (edge_cot_all, node_back_all, halo_back_all) = lax.scan(backward_one, initial, (edge_in_all, node_in_all, received, halo_count, senders, receivers, edge_cot_all, node_cot_all))
        node_back_all = node_back_all + scatter_back(halo_back_all, send_index, node_count)
        node_cot_all = node_back_all.astype(jnp.bfloat16)
        layer_grads[layer_index] = totals
    grad_scale = (N_DOM * N_GROUP * node_count) ** (-0.5)
    stacked = tuple((jnp.stack([layer_grads[layer_index][member] for layer_index in range(layer_count)]) * grad_scale for member in range(6)))
    return (node_all, node_cot_all, edge_cot_all, stacked[0], stacked[1], stacked[2], stacked[3], stacked[4], stacked[5])
```

```python
import functools

import jax
import jax.numpy as jnp
from jax import lax
from jax.experimental import pallas as pl
from jax.experimental.pallas import tpu as pltpu
from jax.sharding import PartitionSpec as P

F32 = jnp.float32
BF16 = jnp.bfloat16
MESH = pl.DeviceIdType.MESH
VMEM_MAIN = 58 * 1024 * 1024


def mm(a, b):
    return lax.dot_general(a, b, (((1,), (0,)), ((), ())), preferred_element_type=F32)


def mm_nt(a, b):
    return lax.dot_general(a, b, (((1,), (1,)), ((), ())), preferred_element_type=F32)


def norm_parts(values):
    centre = values - jnp.mean(values, axis=0, keepdims=True)
    spread = jnp.mean(centre * centre, axis=0, keepdims=True)
    inv = lax.rsqrt(spread + 1e-05)
    return centre * inv, inv


def norm_back(cot, gain_col, hat, inv):
    u = cot * gain_col
    uh = u * hat
    back = inv * (
        u
        - jnp.mean(u, axis=0, keepdims=True)
        - hat * jnp.mean(uh, axis=0, keepdims=True)
    )
    return back, uh


def silu_half(half):
    t = jnp.tanh(half)
    a = 1.0 + t
    h = half * a
    return h.astype(BF16), a + h * (1.0 - t)


def halved(x):
    return (x.astype(F32) * 0.5).astype(BF16)


def wide(tile, width):
    return jnp.concatenate([tile] * (width // tile.shape[1]), axis=1)


def kernel(
    dims,
    cnt_h,
    nodes_h,
    edges_h,
    ncot_h,
    sidx_h,
    snd_h,
    rcv_h,
    w1_h,
    w2_h,
    n1_h,
    n2_h,
    bias_h,
    gain_h,
    x_out,
    x_grad,
    e_grad,
    sum_n,
    sum_e,
    rhs,
    o_x,
    own_l,
    halo_l,
    tab,
    tab_h,
    e_t,
    hid,
    slope,
    hat,
    inv,
    jn,
    nhid,
    nslope,
    nhat,
    ninv,
    cols,
    w1_t,
    w1_sq,
    w2_t,
    w2_b,
    n1_t,
    n2_t,
    n2_b,
    dm,
    dp,
    uh,
    cc,
    de,
    dx,
    fsrc,
    bsrc,
    ret,
    grads_n,
    buf_an,
    buf_bn,
    grads_e,
    buf_ae,
    buf_be,
    fs,
    fr,
    bs,
    br,
    a_s,
    a_r,
    b_s,
    b_r,
    c_s,
    c_r,
    cnt,
    nodes,
    edges,
    ncot,
    sidx,
    snd,
    rcv,
    w1,
    w2,
    n1,
    n2,
    bias,
    gain,
    in_sem,
):
    D, G, L, N, E, H, HALO, W, share_n, share_e = dims
    shares = (share_n, share_e)
    grads = (grads_n, grads_e)
    buf_a = (buf_an, buf_ae)
    buf_b = (buf_bn, buf_be)
    gat = (sum_n, sum_e)
    loads = [
        pltpu.make_async_copy(src, dst, in_sem.at[i])
        for i, (src, dst) in enumerate(
            (
                (nodes_h, nodes),
                (sidx_h, sidx),
                (snd_h, snd),
                (rcv_h, rcv),
                (cnt_h, cnt),
                (edges_h, edges),
                (w1_h, w1),
                (w2_h, w2),
                (bias_h, bias),
                (gain_h, gain),
                (n1_h, n1),
                (n2_h, n2),
                (ncot_h, ncot),
            )
        )
    ]
    for load in loads:
        load.start()
    d = lax.axis_index("dom")
    g = lax.axis_index("group")

    has_up = d + 1 < D
    has_down = d > 0
    has_right = g + 1 < G
    has_left = g > 0
    out_ok = (has_up, has_down, has_right, has_left)
    in_ok = (has_down, has_up, has_left, has_right)
    out_dev = ({"dom": d + 1}, {"dom": d - 1}, {"group": g + 1}, {"group": g - 1})
    in_dev = ({"dom": d - 1}, {"dom": d + 1}, {"group": g - 1}, {"group": g + 1})

    def fcopy(l, k):
        return pltpu.make_async_remote_copy(
            src_ref=fsrc.at[l, k],
            dst_ref=tab_h.at[l, k],
            send_sem=fs.at[l, k],
            recv_sem=fr.at[l, k],
            device_id=out_dev[k],
            device_id_type=MESH,
        )

    def bcopy(l, k):
        return pltpu.make_async_remote_copy(
            src_ref=bsrc.at[l, k],
            dst_ref=ret.at[l, k],
            send_sem=bs.at[l, k],
            recv_sem=br.at[l, k],
            device_id=in_dev[k],
            device_id_type=MESH,
        )

    def send_halo(l):
        for k in range(4):
            @pl.when(out_ok[k])
            def _(k=k):
                fcopy(l, k).start()

    def wait_halo(l):
        for k in range(4):
            @pl.when(in_ok[k])
            def _(k=k):
                fcopy(l, k).wait_recv()

    def send_ret(l):
        for k in range(4):
            @pl.when(in_ok[k])
            def _(k=k):
                bcopy(l, k).start()

    def wait_ret(l):
        for k in range(4):
            @pl.when(out_ok[k])
            def _(k=k):
                bcopy(l, k).wait_recv()

    def a_copy(t, l, off):
        peer = lax.rem(d + off, D)
        return pltpu.make_async_remote_copy(
            src_ref=grads[t].at[l, peer],
            dst_ref=buf_a[t].at[l, off - 1],
            send_sem=a_s.at[t, l, off - 1],
            recv_sem=a_r.at[t, l, off - 1],
            device_id={"dom": peer},
            device_id_type=MESH,
        )

    def b_copy(t, l, off):
        return pltpu.make_async_remote_copy(
            src_ref=buf_b[t].at[l, g],
            dst_ref=buf_b[t].at[l, g],
            send_sem=b_s.at[t, l, off - 1],
            recv_sem=b_r.at[t, l, off - 1],
            device_id={"group": lax.rem(g + off, G)},
            device_id_type=MESH,
        )

    def c_copy(t, l, off):
        return pltpu.make_async_remote_copy(
            src_ref=gat[t].at[l, d],
            dst_ref=gat[t].at[l, d],
            send_sem=c_s.at[t, l, off - 1],
            recv_sem=c_r.at[t, l, off - 1],
            device_id={"dom": lax.rem(d + off, D)},
            device_id_type=MESH,
        )

    def start_a(t, l, pieces):
        rows = sum(p.shape[0] for p in pieces)
        pad = jnp.zeros((D * shares[t] - rows, H), F32)
        whole = jnp.concatenate(list(pieces) + [pad], axis=0)
        grads[t][l] = whole.reshape(D, shares[t], H).astype(BF16)
        for off in range(1, D):
            a_copy(t, l, off).start()

    def start_b(t, l):
        acc = grads[t][l, d].astype(F32)
        for off in range(1, D):
            a_copy(t, l, off).wait_recv()
            acc = acc + buf_a[t][l, off - 1].astype(F32)
        buf_b[t][l, g] = acc.astype(BF16)
        for off in range(1, G):
            b_copy(t, l, off).start()

    def start_c(t, l):
        for off in range(1, G):
            b_copy(t, l, off).wait_recv()
        acc = buf_b[t][l, 0].astype(F32)
        for i in range(1, G):
            acc = acc + buf_b[t][l, i].astype(F32)
        gat[t][l, d] = acc.astype(BF16)
        for off in range(1, D):
            c_copy(t, l, off).start()

    def end_c(t, l):
        for off in range(1, D):
            c_copy(t, l, off).wait_recv()

    for l in range(L):
        for k in range(4):
            tab_h[l, k] = jnp.zeros((H, HALO), BF16)
            ret[l, k] = jnp.zeros((H, HALO), BF16)
    barrier = pltpu.get_barrier_semaphore()
    for off in range(1, D):
        pl.semaphore_signal(
            barrier, inc=1, device_id={"dom": lax.rem(d + off, D)}, device_id_type=MESH
        )
    for off in range(1, G):
        pl.semaphore_signal(
            barrier, inc=1, device_id={"group": lax.rem(g + off, G)}, device_id_type=MESH
        )

    def one_hot(row, ref, row0, height, col0):
        width = row.shape[1]
        sub = lax.broadcasted_iota(jnp.int16, (128, width), 0)
        for j in range(height // 128):
            at = (row - 128 * j).astype(jnp.int16)
            ref[row0 + j * 128 : row0 + (j + 1) * 128, col0 : col0 + width] = jnp.where(
                at == sub, BF16(1), BF16(0)
            )

    def halo_out(l, x_t):
        sent = mm(x_t, o_x[...]).astype(BF16)
        for k in range(4):
            fsrc[l, k] = sent[:, k * HALO : (k + 1) * HALO]

    loads[0].wait()
    loads[1].wait()
    x_t = nodes[0].T
    tab[0] = x_t
    for k in range(4):
        one_hot(sidx[0, k : k + 1, :], o_x, 0, N, k * HALO)
    halo_out(0, x_t)
    pl.semaphore_wait(barrier, D - 1 + G - 1)
    send_halo(0)

    for load in loads[2:5]:
        load.wait()
    sids = snd[...]
    past = sids - N
    edge_0 = cnt[0, 0]
    edge_1 = edge_0 + cnt[0, 1]
    edge_2 = edge_1 + cnt[0, 2]
    sids = (
        sids
        + jnp.where(past >= edge_0, HALO - cnt[0, 0], 0)
        + jnp.where(past >= edge_1, HALO - cnt[0, 1], 0)
        + jnp.where(past >= edge_2, HALO - cnt[0, 2], 0)
    )
    rids = rcv[...]
    RQ, RS, RH = H, H + N, H + 2 * N
    TOP = RH + 4 * HALO
    one_hot(rids, rhs, RQ, N, 0)
    one_hot(sids, rhs, RS, N + 4 * HALO, 0)

    for load in loads[5:]:
        load.wait()
    first = edges[0].T
    e_t[0] = first
    rhs[:H, :] = first

    def column(row):
        return jnp.broadcast_to(row, (128, H)).T

    for l in range(L):
        for j in range(3):
            w1_t[l, j] = halved(w1[l, j * H : (j + 1) * H, :].T)
        w1_sq[l, :, :H] = w1[l, 2 * H :, :]
        w1_sq[l, :, H:] = w1[l, H : 2 * H, :]
        w2_t[l] = w2[l].T
        w2_b[l] = halved(w2[l])
        n1_t[l] = halved(n1[l].T)
        n2_t[l] = n2[l].T
        n2_b[l] = halved(n2[l])
        for j in range(4):
            cols[l, j] = column(bias[l, j : j + 1, :] * (1.0 if j % 2 else 0.5))
        for j in range(2):
            cols[l, 4 + j] = column(gain[l, j : j + 1, :])

    def own_part(l):
        x_t = tab[l]
        own_l[:, :H] = w1_t[l, 0]
        own_l[:, H : H + N] = mm(w1_t[l, 2], x_t).astype(BF16)
        own_l[:, H + N :] = mm(w1_t[l, 1], x_t).astype(BF16)
        for i in range(E // W):
            part = slice(i * W, (i + 1) * W)
            slope[l, :, part] = mm(own_l[...], rhs[:RH, part]) + wide(cols[l, 0], W)

    for l in range(L):
        own_part(l)
        wait_halo(l)
        for k in range(4):
            halo_l[:, k * HALO : (k + 1) * HALO] = mm(w1_t[l, 1], tab_h[l, k]).astype(BF16)

        for i in range(E // W):
            part = slice(i * W, (i + 1) * W)
            h_b, sl = silu_half(slope[l, :, part] + mm(halo_l[...], rhs[RH:, part]))
            hid[l, :, part] = h_b
            slope[l, :, part] = sl
            hat_c, inv_c = norm_parts(mm(w2_t[l], h_b) + wide(cols[l, 1], W))
            hat[l, :, part] = hat_c
            inv[l, :, part] = inv_c
            new = (e_t[l, :, part].astype(F32) + hat_c * wide(cols[l, 4], W)).astype(BF16)
            e_t[l + 1, :, part] = new
            if l + 1 < L:
                rhs[:H, part] = new

        x_t = tab[l]
        joined = jnp.concatenate(
            [x_t, mm_nt(e_t[l + 1], rhs[RQ:RS, :]).astype(BF16)], axis=0
        )
        jn[l] = joined
        h_b, sl = silu_half(mm(n1_t[l], joined) + wide(cols[l, 2], N))
        nhid[l] = h_b
        nslope[l] = sl
        hat_c, inv_c = norm_parts(mm(n2_t[l], h_b) + wide(cols[l, 3], N))
        nhat[l] = hat_c
        ninv[l] = inv_c
        x_new = (x_t.astype(F32) + hat_c * wide(cols[l, 5], N)).astype(BF16)
        if l + 1 < L:
            tab[l + 1] = x_new
            halo_out(l + 1, x_new)
            send_halo(l + 1)
        else:
            x_out[0] = x_new.T

    ones_n = jnp.ones((8, N), BF16)
    ones_e = jnp.ones((8, E), BF16)
    for l in reversed(range(L)):
        cot = ncot[0].T.astype(F32) if l == L - 1 else x_cot.astype(F32)
        dmn, nuh = norm_back(cot, wide(cols[l, 5], N), nhat[l], ninv[l])
        dmn = dmn.astype(BF16)
        dpn = (mm(n2_b[l], dmn) * nslope[l]).astype(BF16)
        djn = mm(n1[l], dpn)
        dx[...] = cot + djn[:H, :]
        dab = djn[H:, :].astype(BF16)
        start_a(
            0,
            l,
            [
                mm_nt(jn[l], dpn),
                mm_nt(nhid[l], dmn),
                mm_nt(ones_n, dpn)[:1],
                mm_nt(ones_n, dmn)[:1],
                mm_nt(ones_n, nuh.astype(BF16))[:1] / gain[l, 1:2, :],
            ],
        )
        if l + 1 < L:
            start_b(0, l + 1)

        for i in range(E // W):
            part = slice(i * W, (i + 1) * W)
            c = mm(dab, rhs[RQ:RS, part])
            if l < L - 1:
                c = c + de[:, part].astype(F32)
            dm_c, uh_c = norm_back(c, wide(cols[l, 4], W), hat[l, :, part], inv[l, :, part])
            uh[:, part] = uh_c.astype(BF16)
            dm_b = dm_c.astype(BF16)
            dm[:, part] = dm_b
            dp_b = (mm(w2_b[l], dm_b) * slope[l, :, part]).astype(BF16)
            dp[:, part] = dp_b
            if l > 0:
                de[:, part] = (c + mm(w1[l, :H, :], dp_b)).astype(BF16)
            else:
                cc[:, part] = c

        def halo_cots(u_h, l=l):
            for k in range(4):
                bsrc[l, k] = mm(
                    w1[l, H : 2 * H, :], u_h[:, k * HALO : (k + 1) * HALO]
                ).astype(BF16)
            send_ret(l)

        u_h = mm_nt(dp[...], rhs[RH:, :]).astype(BF16)
        if l > 0:
            halo_cots(u_h)
        if l + 1 < L:
            start_b(1, l + 1)
        u_o = mm_nt(dp[...], rhs[RQ:RH, :]).astype(BF16)
        halos = jnp.concatenate([tab_h[l, k] for k in range(4)], axis=1)
        start_a(
            1,
            l,
            [
                mm_nt(e_t[l], dp[...]),
                mm_nt(tab[l], u_o[:, N:]) + mm_nt(halos, u_h),
                mm_nt(tab[l], u_o[:, :N]),
                mm_nt(hid[l], dm[...]),
                mm_nt(ones_e, dp[...])[:1],
                mm_nt(ones_e, dm[...])[:1],
                mm_nt(ones_e, uh[...])[:1] / gain[l, 0:1, :],
            ],
        )
        if l == 0:
            start_b(0, 0)
            halo_cots(u_h)
        if l + 1 < L:
            start_c(0, l + 1)
            start_c(1, l + 1)
        total = dx[...] + mm(
            w1_sq[l], jnp.concatenate([u_o[:, :N], u_o[:, N:]], axis=0)
        )
        if l == 0:
            for i in range(E // W):
                part = slice(i * W, (i + 1) * W)
                back = (cc[:, part] + mm(w1[l, :H, :], dp[:, part])).astype(BF16)
                e_grad[0, part, :] = back.T
        wait_ret(l)
        back_in = jnp.concatenate([ret[l, k] for k in range(4)], axis=1)
        x_cot = (total + mm_nt(back_in, o_x[...])).astype(BF16)
    x_grad[0] = x_cot.T

    start_c(0, 0)
    start_b(1, 0)
    start_c(1, 0)
    for l in reversed(range(L)):
        for t in range(2):
            end_c(t, l)

    for l in range(L):
        for k in range(4):
            @pl.when(out_ok[k])
            def _(k=k, l=l):
                fcopy(l, k).wait_send()

            @pl.when(in_ok[k])
            def _(k=k, l=l):
                bcopy(l, k).wait_send()
        for t in range(2):
            for off in range(1, D):
                a_copy(t, l, off).wait_send()
                c_copy(t, l, off).wait_send()
            for off in range(1, G):
                b_copy(t, l, off).wait_send()


def finish(scale, H, x0, xg0, eg0, sum_n, sum_e, x1, xg1, eg1, g_w1, g_w2, g_n1, g_n2, g_b, g_g):
    x1[...] = x0[...]
    xg1[...] = xg0[...]
    eg1[...] = eg0[...]
    L, D, share_n, _ = sum_n.shape
    share_e = sum_e.shape[2]
    for l in range(L):
        node = (sum_n[l].astype(F32) * scale).reshape(D * share_n, H)
        edge = (sum_e[l].astype(F32) * scale).reshape(D * share_e, H)
        g_n1[l] = node[: 2 * H]
        g_n2[l] = node[2 * H : 3 * H]
        g_w1[l] = edge[: 3 * H]
        g_w2[l] = edge[3 * H : 4 * H]
        node = node[3 * H : 3 * H + 8]
        edge = edge[4 * H : 4 * H + 8]
        g_b[l, 0:2, :] = edge[0:2]
        g_b[l, 2:4, :] = node[0:2]
        g_g[l, 0:1, :] = edge[2:3]
        g_g[l, 1:2, :] = node[2:3]


def shards(D, G, nodes, edges, node_cot, send_index, halo_count, senders, receivers, *weights):
    edge_in_w, edge_out_w, node_in_w, node_out_w, biases, gains = weights
    _, N, H = nodes.shape
    E = edges.shape[1]
    L = edge_in_w.shape[0]
    HALO = send_index.shape[2]
    W = 256
    share_n = -(-(3 * H + 3) // (8 * D)) * 8
    share_e = -(-(4 * H + 3) // (8 * D)) * 8
    dims = (D, G, L, N, E, H, HALO, W, share_n, share_e)
    T = N + 4 * HALO
    own_shape = (
        pltpu.VMEM(nodes.shape, BF16),
        pltpu.VMEM(nodes.shape, BF16),
        pltpu.VMEM(edges.shape, BF16),
        pltpu.VMEM((L, D, share_n, H), BF16),
        pltpu.VMEM((L, D, share_e, H), BF16),
    )
    out_shape = (
        jax.ShapeDtypeStruct(nodes.shape, BF16),
        jax.ShapeDtypeStruct(nodes.shape, BF16),
        jax.ShapeDtypeStruct(edges.shape, BF16),
        jax.ShapeDtypeStruct(edge_in_w.shape, F32),
        jax.ShapeDtypeStruct(edge_out_w.shape, F32),
        jax.ShapeDtypeStruct(node_in_w.shape, F32),
        jax.ShapeDtypeStruct(node_out_w.shape, F32),
        jax.ShapeDtypeStruct(biases.shape, F32),
        jax.ShapeDtypeStruct(gains.shape, F32),
    )
    V = pltpu.VMEM
    dma = pltpu.SemaphoreType.DMA
    scratch = [
        V((H + N + T, E), BF16),
        V((N, 4 * HALO), BF16),
        V((H, H + 2 * N), BF16),
        V((H, 4 * HALO), BF16),
        V((L, H, N), BF16),
        V((L, 4, H, HALO), BF16),
        V((L + 1, H, E), BF16),
        V((L, H, E), BF16),
        V((L, H, E), F32),
        V((L, H, E), F32),
        V((L, 1, E), F32),
        V((L, 2 * H, N), BF16),
        V((L, H, N), BF16),
        V((L, H, N), F32),
        V((L, H, N), F32),
        V((L, 1, N), F32),
        V((L, 6, H, 128), F32),
        V((L, 3, H, H), BF16),
        V((L, H, 2 * H), BF16),
        V((L, H, H), BF16),
        V((L, H, H), BF16),
        V((L, H, 2 * H), BF16),
        V((L, H, H), BF16),
        V((L, H, H), BF16),
        V((H, E), BF16),
        V((H, E), BF16),
        V((H, E), BF16),
        V((H, E), F32),
        V((H, E), BF16),
        V((H, N), F32),
        V((L, 4, H, HALO), BF16),
        V((L, 4, H, HALO), BF16),
        V((L, 4, H, HALO), BF16),
        V((L, D, share_n, H), BF16),
        V((L, max(D - 1, 1), share_n, H), BF16),
        V((L, G, share_n, H), BF16),
        V((L, D, share_e, H), BF16),
        V((L, max(D - 1, 1), share_e, H), BF16),
        V((L, G, share_e, H), BF16),
        dma((L, 4)),
        dma((L, 4)),
        dma((L, 4)),
        dma((L, 4)),
        dma((2, L, D)),
        dma((2, L, D)),
        dma((2, L, G)),
        dma((2, L, G)),
        dma((2, L, D)),
        dma((2, L, D)),
        pltpu.SMEM(halo_count.shape, jnp.int32),
    ]
    operands = (nodes, edges, node_cot, send_index, senders, receivers) + weights
    scratch += [V(x.shape, x.dtype) for x in operands] + [dma((13,))]
    vm = pl.BlockSpec(memory_space=pltpu.VMEM)
    hbm = pl.BlockSpec(memory_space=pltpu.HBM)
    own = pl.pallas_call(
        functools.partial(kernel, dims),
        out_shape=own_shape,
        in_specs=[hbm] * 13,
        out_specs=tuple([vm] * 5),
        scratch_shapes=scratch,
        compiler_params=pltpu.CompilerParams(
            collective_id=0, has_side_effects=True, vmem_limit_bytes=VMEM_MAIN
        ),
    )(
        halo_count,
        *operands,
    )
    scale = (D * G * N) ** (-0.5)
    return pl.pallas_call(
        functools.partial(finish, scale, H),
        out_shape=out_shape,
        in_specs=[vm] * 5,
        out_specs=tuple([vm] * 9),
        compiler_params=pltpu.CompilerParams(vmem_limit_bytes=8 * 1024 * 1024),
    )(*own)


def solution(mesh):
    part3 = P(("dom", "group"), None, None)
    part2 = P(("dom", "group"), None)
    in_specs = (part3, part3, part3, part3, part2, part2, part2) + (P(),) * 6
    out_specs = (part3, part3, part3) + (P(),) * 6
    body = functools.partial(shards, mesh.shape["dom"], mesh.shape["group"])
    return jax.shard_map(
        body, mesh=mesh, in_specs=in_specs, out_specs=out_specs, check_vma=False
    )
```

```python
import functools

import jax
import jax.numpy as jnp
from jax import lax
from jax.experimental import pallas as pl
from jax.experimental.pallas import tpu as pltpu
from jax.sharding import PartitionSpec as P

F32 = jnp.float32
BF16 = jnp.bfloat16
MESH = pl.DeviceIdType.MESH
VMEM_MAIN = 58 * 1024 * 1024


def mm(a, b):
    return lax.dot_general(a, b, (((1,), (0,)), ((), ())), preferred_element_type=F32)


def mm_nt(a, b):
    return lax.dot_general(a, b, (((1,), (1,)), ((), ())), preferred_element_type=F32)


def norm_parts(values):
    centre = values - jnp.mean(values, axis=0, keepdims=True)
    spread = jnp.mean(centre * centre, axis=0, keepdims=True)
    inv = lax.rsqrt(spread + 1e-05)
    return centre * inv, inv


def norm_back(cot, gain_col, hat, inv):
    u = cot * gain_col
    uh = u * hat
    back = inv * (
        u
        - jnp.mean(u, axis=0, keepdims=True)
        - hat * jnp.mean(uh, axis=0, keepdims=True)
    )
    return back, uh


def fold(x):
    total = x[:, :128]
    for i in range(1, x.shape[1] // 128):
        total = total + x[:, i * 128 : (i + 1) * 128]
    return total


def lane_sum(x):
    return jnp.sum(x.T, axis=0, keepdims=True)


def silu_half(half):
    t = jnp.tanh(half)
    a = 1.0 + t
    h = half * a
    return h.astype(BF16), a + h * (1.0 - t)


def halved(x):
    return (x.astype(F32) * 0.5).astype(BF16)


def wide(tile, width):
    return jnp.concatenate([tile] * (width // tile.shape[1]), axis=1)


def kernel(
    dims,
    cnt_h,
    nodes_h,
    edges_h,
    ncot_h,
    sidx_h,
    snd_h,
    rcv_h,
    w1_h,
    w2_h,
    n1_h,
    n2_h,
    bias_h,
    gain_h,
    x_out,
    x_grad,
    e_grad,
    sum_n,
    sum_e,
    rhs,
    o_x,
    own_l,
    halo_l,
    tab,
    tab_h,
    oh,
    stk,
    e_last,
    hid,
    slope,
    hat,
    inv,
    jn,
    nhid,
    nslope,
    nhat,
    ninv,
    cols,
    w1_t,
    w1_sq,
    w2_t,
    w2_b,
    n1_t,
    n2_t,
    n2_b,
    dm,
    dp,
    cc,
    de,
    dx,
    fsrc,
    bsrc,
    ret,
    grads_n,
    buf_an,
    buf_bn,
    grads_e,
    buf_ae,
    buf_be,
    fs,
    fr,
    bs,
    br,
    a_s,
    a_r,
    b_s,
    b_r,
    c_s,
    c_r,
    cnt,
    nodes,
    edges,
    ncot,
    sidx,
    snd,
    rcv,
    w1,
    w2,
    n1,
    n2,
    bias,
    gain,
    in_sem,
):
    D, G, L, N, E, H, HALO, W, share_n, share_e = dims
    shares = (share_n, share_e)
    grads = (grads_n, grads_e)
    buf_a = (buf_an, buf_ae)
    buf_b = (buf_bn, buf_be)
    gat = (sum_n, sum_e)
    loads = [
        pltpu.make_async_copy(src, dst, in_sem.at[i])
        for i, (src, dst) in enumerate(
            (
                (nodes_h, nodes),
                (sidx_h, sidx),
                (snd_h, snd),
                (rcv_h, rcv),
                (cnt_h, cnt),
                (edges_h, edges),
                (w1_h, w1),
                (w2_h, w2),
                (bias_h, bias),
                (gain_h, gain),
                (n1_h, n1),
                (n2_h, n2),
                (ncot_h, ncot),
            )
        )
    ]
    for load in loads:
        load.start()
    d = lax.axis_index("dom")
    g = lax.axis_index("group")

    has_up = d + 1 < D
    has_down = d > 0
    has_right = g + 1 < G
    has_left = g > 0
    out_ok = (has_up, has_down, has_right, has_left)
    in_ok = (has_down, has_up, has_left, has_right)
    out_dev = ({"dom": d + 1}, {"dom": d - 1}, {"group": g + 1}, {"group": g - 1})
    in_dev = ({"dom": d - 1}, {"dom": d + 1}, {"group": g - 1}, {"group": g + 1})

    def fcopy(l, k):
        return pltpu.make_async_remote_copy(
            src_ref=fsrc.at[l, k],
            dst_ref=tab_h.at[l, k],
            send_sem=fs.at[l, k],
            recv_sem=fr.at[l, k],
            device_id=out_dev[k],
            device_id_type=MESH,
        )

    def bcopy(l, k):
        return pltpu.make_async_remote_copy(
            src_ref=bsrc.at[l, k],
            dst_ref=ret.at[l, k],
            send_sem=bs.at[l, k],
            recv_sem=br.at[l, k],
            device_id=in_dev[k],
            device_id_type=MESH,
        )

    def send_halo(l):
        for k in range(4):
            @pl.when(out_ok[k])
            def _(k=k):
                fcopy(l, k).start()

    def wait_halo(l):
        for k in range(4):
            @pl.when(in_ok[k])
            def _(k=k):
                fcopy(l, k).wait_recv()

    def send_ret(l):
        for k in range(4):
            @pl.when(in_ok[k])
            def _(k=k):
                bcopy(l, k).start()

    def wait_ret(l):
        for k in range(4):
            @pl.when(out_ok[k])
            def _(k=k):
                bcopy(l, k).wait_recv()

    def a_copy(t, l, off):
        peer = lax.rem(d + off, D)
        return pltpu.make_async_remote_copy(
            src_ref=grads[t].at[l, peer],
            dst_ref=buf_a[t].at[l, off - 1],
            send_sem=a_s.at[t, l, off - 1],
            recv_sem=a_r.at[t, l, off - 1],
            device_id={"dom": peer},
            device_id_type=MESH,
        )

    def b_copy(t, l, off):
        return pltpu.make_async_remote_copy(
            src_ref=buf_b[t].at[l, g],
            dst_ref=buf_b[t].at[l, g],
            send_sem=b_s.at[t, l, off - 1],
            recv_sem=b_r.at[t, l, off - 1],
            device_id={"group": lax.rem(g + off, G)},
            device_id_type=MESH,
        )

    def c_copy(t, l, off):
        return pltpu.make_async_remote_copy(
            src_ref=gat[t].at[l, d],
            dst_ref=gat[t].at[l, d],
            send_sem=c_s.at[t, l, off - 1],
            recv_sem=c_r.at[t, l, off - 1],
            device_id={"dom": lax.rem(d + off, D)},
            device_id_type=MESH,
        )

    def start_a(t, l, pieces):
        rows = sum(p.shape[0] for p in pieces)
        pad = jnp.zeros((D * shares[t] - rows, H), F32)
        whole = jnp.concatenate(list(pieces) + [pad], axis=0)
        grads[t][l] = whole.reshape(D, shares[t], H).astype(BF16)
        for off in range(1, D):
            a_copy(t, l, off).start()

    def start_b(t, l):
        acc = grads[t][l, d].astype(F32)
        for off in range(1, D):
            a_copy(t, l, off).wait_recv()
            acc = acc + buf_a[t][l, off - 1].astype(F32)
        buf_b[t][l, g] = acc.astype(BF16)
        for off in range(1, G):
            b_copy(t, l, off).start()

    def start_c(t, l):
        for off in range(1, G):
            b_copy(t, l, off).wait_recv()
        acc = buf_b[t][l, 0].astype(F32)
        for i in range(1, G):
            acc = acc + buf_b[t][l, i].astype(F32)
        gat[t][l, d] = acc.astype(BF16)
        for off in range(1, D):
            c_copy(t, l, off).start()

    def end_c(t, l):
        for off in range(1, D):
            c_copy(t, l, off).wait_recv()

    for l in range(L):
        for k in range(4):
            tab_h[l, k] = jnp.zeros((H, HALO), BF16)
            ret[l, k] = jnp.zeros((H, HALO), BF16)
    barrier = pltpu.get_barrier_semaphore()
    for off in range(1, D):
        pl.semaphore_signal(
            barrier, inc=1, device_id={"dom": lax.rem(d + off, D)}, device_id_type=MESH
        )
    for off in range(1, G):
        pl.semaphore_signal(
            barrier, inc=1, device_id={"group": lax.rem(g + off, G)}, device_id_type=MESH
        )

    def one_hot(row, ref, row0, height, col0):
        width = row.shape[1]
        sub = lax.broadcasted_iota(jnp.int16, (128, width), 0)
        for j in range(height // 128):
            at = (row - 128 * j).astype(jnp.int16)
            ref[row0 + j * 128 : row0 + (j + 1) * 128, col0 : col0 + width] = jnp.where(
                at == sub, BF16(1), BF16(0)
            )

    def spread(row):
        return jnp.broadcast_to(row, (128, row.shape[1])).T

    def one_hot_rows(ids, height, col0):
        lane = lax.broadcasted_iota(jnp.int16, (W, 128), 1)
        for i in range(E // W):
            at = spread(ids[:, i * W : (i + 1) * W]).astype(jnp.int16)
            for j in range(height // 128):
                oh[i * W : (i + 1) * W, col0 + j * 128 : col0 + (j + 1) * 128] = jnp.where(
                    at - jnp.int16(128 * j) == lane, BF16(1), BF16(0)
                )

    def halo_out(l, x_t):
        sent = mm(x_t, o_x[...]).astype(BF16)
        for k in range(4):
            fsrc[l, k] = sent[:, k * HALO : (k + 1) * HALO]

    loads[0].wait()
    loads[1].wait()
    x_t = nodes[0].T
    tab[0] = x_t
    for k in range(4):
        one_hot(sidx[0, k : k + 1, :], o_x, 0, N, k * HALO)
    halo_out(0, x_t)
    pl.semaphore_wait(barrier, D - 1 + G - 1)
    send_halo(0)

    for load in loads[2:5]:
        load.wait()
    sids = snd[...]
    past = sids - N
    edge_0 = cnt[0, 0]
    edge_1 = edge_0 + cnt[0, 1]
    edge_2 = edge_1 + cnt[0, 2]
    sids = (
        sids
        + jnp.where(past >= edge_0, HALO - cnt[0, 0], 0)
        + jnp.where(past >= edge_1, HALO - cnt[0, 1], 0)
        + jnp.where(past >= edge_2, HALO - cnt[0, 2], 0)
    )
    rids = rcv[...]
    RQ, RS, RH = H, H + N, H + 2 * N
    TOP = RH + 4 * HALO
    one_hot(rids, rhs, RQ, N, 0)
    one_hot(sids, rhs, RS, N + 4 * HALO, 0)

    for load in loads[5:]:
        load.wait()
    first = edges[0].T
    stk[0, :H, :] = first
    rhs[:H, :] = first

    def column(row):
        return jnp.broadcast_to(row, (128, H)).T

    for l in range(L):
        for j in range(3):
            w1_t[l, j] = halved(w1[l, j * H : (j + 1) * H, :].T)
        w1_sq[l, :, :H] = w1[l, 2 * H :, :]
        w1_sq[l, :, H:] = w1[l, H : 2 * H, :]
        w2_t[l] = w2[l].T
        w2_b[l] = halved(w2[l])
        n1_t[l] = halved(n1[l].T)
        n2_t[l] = n2[l].T
        n2_b[l] = halved(n2[l])
        for j in range(4):
            cols[l, j] = column(bias[l, j : j + 1, :] * (1.0 if j % 2 else 0.5))
        for j in range(2):
            cols[l, 4 + j] = column(gain[l, j : j + 1, :])

    def own_part(l):
        x_t = tab[l]
        own_l[:, :H] = w1_t[l, 0]
        own_l[:, H : H + N] = mm(w1_t[l, 2], x_t).astype(BF16)
        own_l[:, H + N :] = mm(w1_t[l, 1], x_t).astype(BF16)
        for i in range(E // W):
            part = slice(i * W, (i + 1) * W)
            slope[l, :, part] = mm(own_l[...], rhs[:RH, part]) + wide(cols[l, 0], W)

    for l in range(L):
        stk[l, H : H + 16, :] = jnp.ones((16, E), BF16)
        hid[l, H:, :] = jnp.ones((16, E), BF16)
    one_hot_rows(rids, N, 0)

    def halo_rows(l):
        return jnp.concatenate([tab_h[l, k] for k in range(4)], axis=1)

    for l in range(L):
        own_part(l)
        if l == L - 1:
            if l > 0:
                halos = halo_rows(0)
                stk[0, H + 16 : 2 * H + 16, :] = (
                    mm(tab[0], rhs[RS:RH, :]) + mm(halos, rhs[RH:, :])
                ).astype(BF16)
                stk[0, 2 * H + 16 :, :] = mm(tab[0], rhs[RQ:RS, :]).astype(BF16)
            one_hot_rows(sids, N + 4 * HALO, N)
        wait_halo(l)
        if l == L - 1 and l == 0:
            halos = halo_rows(0)
            stk[0, H + 16 : 2 * H + 16, :] = (
                mm(tab[0], rhs[RS:RH, :]) + mm(halos, rhs[RH:, :])
            ).astype(BF16)
            stk[0, 2 * H + 16 :, :] = mm(tab[0], rhs[RQ:RS, :]).astype(BF16)
        for k in range(4):
            halo_l[:, k * HALO : (k + 1) * HALO] = mm(w1_t[l, 1], tab_h[l, k]).astype(BF16)

        def hidden(i, l=l):
            part = slice(i * W, (i + 1) * W)
            h_b, sl = silu_half(slope[l, :, part] + mm(halo_l[...], rhs[RH:, part]))
            hid[l, :H, part] = h_b
            slope[l, :, part] = sl

        def update(i, l=l):
            part = slice(i * W, (i + 1) * W)
            hat_c, inv_c = norm_parts(mm(w2_t[l], hid[l, :H, part]) + wide(cols[l, 1], W))
            hat[l, :, part] = hat_c
            inv[l, :, part] = inv_c
            new = (stk[l, :H, part].astype(F32) + hat_c * wide(cols[l, 4], W)).astype(BF16)
            if l + 1 < L:
                stk[l + 1, :H, part] = new
                rhs[:H, part] = new
            else:
                e_last[:, part] = new

        for i in range(E // W):
            hidden(i)
        for i in range(E // W):
            update(i)

        x_t = tab[l]
        e_new = stk[l + 1, :H, :] if l + 1 < L else e_last[...]
        joined = jnp.concatenate([x_t, mm(e_new, oh[:, :N]).astype(BF16)], axis=0)
        jn[l] = joined
        h_b, sl = silu_half(mm(n1_t[l], joined) + wide(cols[l, 2], N))
        nhid[l] = h_b
        nslope[l] = sl
        hat_c, inv_c = norm_parts(mm(n2_t[l], h_b) + wide(cols[l, 3], N))
        nhat[l] = hat_c
        ninv[l] = inv_c
        x_new = (x_t.astype(F32) + hat_c * wide(cols[l, 5], N)).astype(BF16)
        if l + 1 < L:
            tab[l + 1] = x_new
            halo_out(l + 1, x_new)
            send_halo(l + 1)
        else:
            x_out[0] = x_new.T

    ones_n = jnp.ones((16, N), BF16)
    for l in reversed(range(L)):
        cot = ncot[0].T.astype(F32) if l == L - 1 else x_cot.astype(F32)
        dmn, nuh = norm_back(cot, wide(cols[l, 5], N), nhat[l], ninv[l])
        dmn = dmn.astype(BF16)
        dpn = (mm(n2_b[l], dmn) * nslope[l]).astype(BF16)
        djn = mm(n1[l], dpn)
        dx[...] = cot + djn[:H, :]
        dab = djn[H:, :].astype(BF16)

        def node_grads(l=l, dpn=dpn, dmn=dmn, nuh=nuh):
            one = mm_nt(jnp.concatenate([jn[l], ones_n], axis=0), dpn)
            two = mm_nt(jnp.concatenate([nhid[l], ones_n], axis=0), dmn)
            start_a(
                0,
                l,
                [
                    one[: 2 * H],
                    two[:H],
                    one[2 * H : 2 * H + 1],
                    two[H : H + 1],
                    lane_sum(fold(nuh)) / gain[l, 1:2, :],
                ],
            )

        dge = jnp.zeros((H, 128), F32)

        def norm_cot(i, dge, l=l, dab=dab):
            part = slice(i * W, (i + 1) * W)
            c = mm(dab, rhs[RQ:RS, part])
            if l < L - 1:
                c = c + de[:, part].astype(F32)
            dm_c, uh_c = norm_back(c, wide(cols[l, 4], W), hat[l, :, part], inv[l, :, part])
            dm[:, part] = dm_c.astype(BF16)
            cc[:, part] = c
            return dge + fold(uh_c)

        def pre_cot(i, l=l):
            part = slice(i * W, (i + 1) * W)
            dp[:, part] = (mm(w2_b[l], dm[:, part]) * slope[l, :, part]).astype(BF16)

        for i in range(E // W):
            dge = norm_cot(i, dge)
        if l == 0:
            node_grads()
        for i in range(E // W):
            pre_cot(i)

        def halo_cots(l=l):
            u_h = mm(dp[...], oh[:, 2 * N :]).astype(BF16)
            for k in range(4):
                bsrc[l, k] = mm(
                    w1[l, H : 2 * H, :], u_h[:, k * HALO : (k + 1) * HALO]
                ).astype(BF16)
            send_ret(l)
            return u_h

        def edge_grads(w1_rows, db1, l=l, dge=dge):
            two = mm_nt(hid[l], dm[...])
            start_a(
                1,
                l,
                w1_rows
                + [two[:H], db1, two[H : H + 1], lane_sum(dge) / gain[l, 0:1, :]],
            )

        if l > 0:
            u_h = halo_cots()
            node_grads()
            for i in range(E // W):
                part = slice(i * W, (i + 1) * W)
                de[:, part] = (cc[:, part] + mm(w1[l, :H, :], dp[:, part])).astype(BF16)
            u_o = mm(dp[...], oh[:, : 2 * N]).astype(BF16)
            one = mm_nt(stk[l, : H + 16, :], dp[...])
            edge_grads(
                [
                    one[:H],
                    mm_nt(tab[l], u_o[:, N:]) + mm_nt(halo_rows(l), u_h),
                    mm_nt(tab[l], u_o[:, :N]),
                ],
                one[H : H + 1],
            )
            if l + 1 < L:
                start_b(0, l + 1)
                start_b(1, l + 1)
                start_c(0, l + 1)
                start_c(1, l + 1)
        else:
            one = mm_nt(stk[0], dp[...])
            edge_grads([one[:H], one[H + 16 :]], one[H : H + 1])
            if L > 1:
                start_b(0, 1)
                start_b(1, 1)
            halo_cots()
            u_o = mm(dp[...], oh[:, : 2 * N]).astype(BF16)
        total = dx[...] + mm(
            w1_sq[l], jnp.concatenate([u_o[:, :N], u_o[:, N:]], axis=0)
        )
        if l == 0:
            for i in range(E // W):
                part = slice(i * W, (i + 1) * W)
                back = (cc[:, part] + mm(w1[l, :H, :], dp[:, part])).astype(BF16)
                e_grad[0, part, :] = back.T
            start_b(1, 0)
            start_b(0, 0)
            if L > 1:
                start_c(0, 1)
                start_c(1, 1)
        wait_ret(l)
        back_in = jnp.concatenate([ret[l, k] for k in range(4)], axis=1)
        x_cot = (total + mm_nt(back_in, o_x[...])).astype(BF16)
    x_grad[0] = x_cot.T

    start_c(1, 0)
    start_c(0, 0)
    for l in reversed(range(L)):
        for t in range(2):
            end_c(t, l)

    for l in range(L):
        for k in range(4):
            @pl.when(out_ok[k])
            def _(k=k, l=l):
                fcopy(l, k).wait_send()

            @pl.when(in_ok[k])
            def _(k=k, l=l):
                bcopy(l, k).wait_send()
        for t in range(2):
            for off in range(1, D):
                a_copy(t, l, off).wait_send()
                c_copy(t, l, off).wait_send()
            for off in range(1, G):
                b_copy(t, l, off).wait_send()


def finish(scale, H, x0, xg0, eg0, sum_n, sum_e, x1, xg1, eg1, g_w1, g_w2, g_n1, g_n2, g_b, g_g):
    x1[...] = x0[...]
    xg1[...] = xg0[...]
    eg1[...] = eg0[...]
    L, D, share_n, _ = sum_n.shape
    share_e = sum_e.shape[2]
    for l in range(L):
        node = (sum_n[l].astype(F32) * scale).reshape(D * share_n, H)
        edge = (sum_e[l].astype(F32) * scale).reshape(D * share_e, H)
        g_n1[l] = node[: 2 * H]
        g_n2[l] = node[2 * H : 3 * H]
        g_w1[l] = edge[: 3 * H]
        g_w2[l] = edge[3 * H : 4 * H]
        node = node[3 * H : 3 * H + 8]
        edge = edge[4 * H : 4 * H + 8]
        g_b[l, 0:2, :] = edge[0:2]
        g_b[l, 2:4, :] = node[0:2]
        g_g[l, 0:1, :] = edge[2:3]
        g_g[l, 1:2, :] = node[2:3]


def shards(D, G, nodes, edges, node_cot, send_index, halo_count, senders, receivers, *weights):
    edge_in_w, edge_out_w, node_in_w, node_out_w, biases, gains = weights
    _, N, H = nodes.shape
    E = edges.shape[1]
    L = edge_in_w.shape[0]
    HALO = send_index.shape[2]
    W = 256
    share_n = -(-(3 * H + 3) // (8 * D)) * 8
    share_e = -(-(4 * H + 3) // (8 * D)) * 8
    dims = (D, G, L, N, E, H, HALO, W, share_n, share_e)
    T = N + 4 * HALO
    own_shape = (
        pltpu.VMEM(nodes.shape, BF16),
        pltpu.VMEM(nodes.shape, BF16),
        pltpu.VMEM(edges.shape, BF16),
        pltpu.VMEM((L, D, share_n, H), BF16),
        pltpu.VMEM((L, D, share_e, H), BF16),
    )
    out_shape = (
        jax.ShapeDtypeStruct(nodes.shape, BF16),
        jax.ShapeDtypeStruct(nodes.shape, BF16),
        jax.ShapeDtypeStruct(edges.shape, BF16),
        jax.ShapeDtypeStruct(edge_in_w.shape, F32),
        jax.ShapeDtypeStruct(edge_out_w.shape, F32),
        jax.ShapeDtypeStruct(node_in_w.shape, F32),
        jax.ShapeDtypeStruct(node_out_w.shape, F32),
        jax.ShapeDtypeStruct(biases.shape, F32),
        jax.ShapeDtypeStruct(gains.shape, F32),
    )
    V = pltpu.VMEM
    dma = pltpu.SemaphoreType.DMA
    scratch = [
        V((H + N + T, E), BF16),
        V((N, 4 * HALO), BF16),
        V((H, H + 2 * N), BF16),
        V((H, 4 * HALO), BF16),
        V((L, H, N), BF16),
        V((L, 4, H, HALO), BF16),
        V((E, T + N), BF16),
        V((L, 3 * H + 16, E), BF16),
        V((H, E), BF16),
        V((L, H + 16, E), BF16),
        V((L, H, E), F32),
        V((L, H, E), F32),
        V((L, 1, E), F32),
        V((L, 2 * H, N), BF16),
        V((L, H, N), BF16),
        V((L, H, N), F32),
        V((L, H, N), F32),
        V((L, 1, N), F32),
        V((L, 6, H, 128), F32),
        V((L, 3, H, H), BF16),
        V((L, H, 2 * H), BF16),
        V((L, H, H), BF16),
        V((L, H, H), BF16),
        V((L, H, 2 * H), BF16),
        V((L, H, H), BF16),
        V((L, H, H), BF16),
        V((H, E), BF16),
        V((H, E), BF16),
        V((H, E), F32),
        V((H, E), BF16),
        V((H, N), F32),
        V((L, 4, H, HALO), BF16),
        V((L, 4, H, HALO), BF16),
        V((L, 4, H, HALO), BF16),
        V((L, D, share_n, H), BF16),
        V((L, max(D - 1, 1), share_n, H), BF16),
        V((L, G, share_n, H), BF16),
        V((L, D, share_e, H), BF16),
        V((L, max(D - 1, 1), share_e, H), BF16),
        V((L, G, share_e, H), BF16),
        dma((L, 4)),
        dma((L, 4)),
        dma((L, 4)),
        dma((L, 4)),
        dma((2, L, D)),
        dma((2, L, D)),
        dma((2, L, G)),
        dma((2, L, G)),
        dma((2, L, D)),
        dma((2, L, D)),
        pltpu.SMEM(halo_count.shape, jnp.int32),
    ]
    operands = (nodes, edges, node_cot, send_index, senders, receivers) + weights
    scratch += [V(x.shape, x.dtype) for x in operands] + [dma((13,))]
    vm = pl.BlockSpec(memory_space=pltpu.VMEM)
    hbm = pl.BlockSpec(memory_space=pltpu.HBM)
    own = pl.pallas_call(
        functools.partial(kernel, dims),
        out_shape=own_shape,
        in_specs=[hbm] * 13,
        out_specs=tuple([vm] * 5),
        scratch_shapes=scratch,
        compiler_params=pltpu.CompilerParams(
            collective_id=0, has_side_effects=True, vmem_limit_bytes=VMEM_MAIN
        ),
    )(
        halo_count,
        *operands,
    )
    scale = (D * G * N) ** (-0.5)
    return pl.pallas_call(
        functools.partial(finish, scale, H),
        out_shape=out_shape,
        in_specs=[vm] * 5,
        out_specs=tuple([vm] * 9),
        compiler_params=pltpu.CompilerParams(vmem_limit_bytes=8 * 1024 * 1024),
    )(*own)


def solution(mesh):
    part3 = P(("dom", "group"), None, None)
    part2 = P(("dom", "group"), None)
    in_specs = (part3, part3, part3, part3, part2, part2, part2) + (P(),) * 6
    out_specs = (part3, part3, part3) + (P(),) * 6
    body = functools.partial(shards, mesh.shape["dom"], mesh.shape["group"])
    return jax.shard_map(
        body, mesh=mesh, in_specs=in_specs, out_specs=out_specs, check_vma=False
    )
```

```python
import functools

import jax
import jax.numpy as jnp
from jax import lax
from jax.experimental import pallas as pl
from jax.experimental.pallas import tpu as pltpu
from jax.sharding import PartitionSpec as P

F32 = jnp.float32
BF16 = jnp.bfloat16
MESH = pl.DeviceIdType.MESH
VMEM_MAIN = 58 * 1024 * 1024


def mm(a, b):
    return lax.dot_general(a, b, (((1,), (0,)), ((), ())), preferred_element_type=F32)


def mm_nt(a, b):
    return lax.dot_general(a, b, (((1,), (1,)), ((), ())), preferred_element_type=F32)


def norm_parts(values):
    spread = jnp.mean(values * values, axis=0, keepdims=True)
    inv = lax.rsqrt(spread + 1e-05)
    return values * inv, inv


def norm_back(cot, gain_col, hat, inv):
    u = cot * gain_col
    uh = u * hat
    back = inv * (
        u
        - jnp.mean(u, axis=0, keepdims=True)
        - hat * jnp.mean(uh, axis=0, keepdims=True)
    )
    return back, uh


def fold(x):
    total = x[:, :128]
    for i in range(1, x.shape[1] // 128):
        total = total + x[:, i * 128 : (i + 1) * 128]
    return total


def lane_sum(x):
    return jnp.sum(x.T, axis=0, keepdims=True)


def silu_half(half):
    t = jnp.tanh(half)
    a = 1.0 + t
    h = half * a
    return h.astype(BF16), a + h * (1.0 - t)


def halved(x):
    return (x.astype(F32) * 0.5).astype(BF16)


def wide(tile, width):
    return jnp.concatenate([tile] * (width // tile.shape[1]), axis=1)


def kernel(
    dims,
    cnt_h,
    nodes_h,
    edges_h,
    ncot_h,
    sidx_h,
    snd_h,
    rcv_h,
    w1_h,
    w2_h,
    n1_h,
    n2_h,
    bias_h,
    gain_h,
    x_out,
    x_grad,
    e_grad,
    sum_n,
    sum_e,
    rhs,
    o_x,
    own_l,
    halo_l,
    tab,
    tab_h,
    oh,
    stk,
    e_last,
    hid,
    slope,
    hat,
    inv,
    jn,
    nhid,
    nslope,
    nhat,
    ninv,
    cols,
    w1_t,
    w1_sq,
    w2_t,
    w2_b,
    n1_t,
    n2_t,
    n2_b,
    dm,
    dp,
    cc,
    de,
    dx,
    fsrc,
    bsrc,
    ret,
    grads_n,
    buf_an,
    buf_bn,
    grads_e,
    buf_ae,
    buf_be,
    fs,
    fr,
    bs,
    br,
    a_s,
    a_r,
    b_s,
    b_r,
    c_s,
    c_r,
    cnt,
    nodes,
    edges,
    ncot,
    sidx,
    snd,
    rcv,
    w1,
    w2,
    n1,
    n2,
    bias,
    gain,
    in_sem,
):
    D, G, L, N, E, H, HALO, W, share_n, share_e = dims
    shares = (share_n, share_e)
    grads = (grads_n, grads_e)
    buf_a = (buf_an, buf_ae)
    buf_b = (buf_bn, buf_be)
    gat = (sum_n, sum_e)
    loads = [
        pltpu.make_async_copy(src, dst, in_sem.at[i])
        for i, (src, dst) in enumerate(
            (
                (nodes_h, nodes),
                (sidx_h, sidx),
                (snd_h, snd),
                (rcv_h, rcv),
                (cnt_h, cnt),
                (edges_h, edges),
                (w1_h, w1),
                (w2_h, w2),
                (bias_h, bias),
                (gain_h, gain),
                (n1_h, n1),
                (n2_h, n2),
                (ncot_h, ncot),
            )
        )
    ]
    for load in loads:
        load.start()
    d = lax.axis_index("dom")
    g = lax.axis_index("group")

    has_up = d + 1 < D
    has_down = d > 0
    has_right = g + 1 < G
    has_left = g > 0
    out_ok = (has_up, has_down, has_right, has_left)
    in_ok = (has_down, has_up, has_left, has_right)
    out_dev = ({"dom": d + 1}, {"dom": d - 1}, {"group": g + 1}, {"group": g - 1})
    in_dev = ({"dom": d - 1}, {"dom": d + 1}, {"group": g - 1}, {"group": g + 1})

    def fcopy(l, k):
        return pltpu.make_async_remote_copy(
            src_ref=fsrc.at[l, k],
            dst_ref=tab_h.at[l, k],
            send_sem=fs.at[l, k],
            recv_sem=fr.at[l, k],
            device_id=out_dev[k],
            device_id_type=MESH,
        )

    def bcopy(l, k):
        return pltpu.make_async_remote_copy(
            src_ref=bsrc.at[l, k],
            dst_ref=ret.at[l, k],
            send_sem=bs.at[l, k],
            recv_sem=br.at[l, k],
            device_id=in_dev[k],
            device_id_type=MESH,
        )

    def send_halo(l):
        for k in range(4):
            @pl.when(out_ok[k])
            def _(k=k):
                fcopy(l, k).start()

    def wait_halo(l):
        for k in range(4):
            @pl.when(in_ok[k])
            def _(k=k):
                fcopy(l, k).wait_recv()

    def send_ret(l):
        for k in range(4):
            @pl.when(in_ok[k])
            def _(k=k):
                bcopy(l, k).start()

    def wait_ret(l):
        for k in range(4):
            @pl.when(out_ok[k])
            def _(k=k):
                bcopy(l, k).wait_recv()

    far_first = sorted(range(1, D), key=lambda off: abs(2 * off - D))

    def a_copy(t, l, off):
        peer = lax.rem(d + off, D)
        return pltpu.make_async_remote_copy(
            src_ref=grads[t].at[l, peer],
            dst_ref=buf_a[t].at[l, off - 1],
            send_sem=a_s.at[t, l],
            recv_sem=a_r.at[t, l],
            device_id={"dom": peer},
            device_id_type=MESH,
        )

    def b_copy(t, l, off):
        return pltpu.make_async_remote_copy(
            src_ref=buf_b[t].at[l, g],
            dst_ref=buf_b[t].at[l, g],
            send_sem=b_s.at[t, l],
            recv_sem=b_r.at[t, l],
            device_id={"group": lax.rem(g + off, G)},
            device_id_type=MESH,
        )

    def c_copy(t, l, off):
        return pltpu.make_async_remote_copy(
            src_ref=gat[t].at[l, d],
            dst_ref=gat[t].at[l, d],
            send_sem=c_s.at[t, l],
            recv_sem=c_r.at[t, l],
            device_id={"dom": lax.rem(d + off, D)},
            device_id_type=MESH,
        )

    def every(ref, send_sem, recv_sem, axis, here, size):
        return pltpu.make_async_remote_copy(
            src_ref=ref,
            dst_ref=ref,
            send_sem=send_sem,
            recv_sem=recv_sem,
            device_id={axis: lax.rem(here + 1, size)},
            device_id_type=MESH,
        )

    def a_all(t, l):
        return every(buf_a[t].at[l, pl.ds(0, D - 1)], a_s.at[t, l], a_r.at[t, l], "dom", d, D)

    def b_all(t, l):
        return every(buf_b[t].at[l, pl.ds(0, G - 1)], b_s.at[t, l], b_r.at[t, l], "group", g, G)

    def c_all(t, l):
        return every(gat[t].at[l, pl.ds(0, D - 1)], c_s.at[t, l], c_r.at[t, l], "dom", d, D)

    def start_a(t, l, pieces):
        rows = sum(p.shape[0] for p in pieces)
        pad = jnp.zeros((D * shares[t] - rows, H), F32)
        whole = jnp.concatenate(list(pieces) + [pad], axis=0)
        grads[t][l] = whole.reshape(D, shares[t], H).astype(BF16)
        for off in far_first:
            a_copy(t, l, off).start()

    def start_b(t, l):
        if D > 1:
            a_all(t, l).wait_recv()
        acc = grads[t][l, d].astype(F32)
        for off in range(1, D):
            acc = acc + buf_a[t][l, off - 1].astype(F32)
        buf_b[t][l, g] = acc.astype(BF16)
        for off in range(1, G):
            b_copy(t, l, off).start()

    def start_c(t, l):
        if G > 1:
            b_all(t, l).wait_recv()
        acc = buf_b[t][l, 0].astype(F32)
        for i in range(1, G):
            acc = acc + buf_b[t][l, i].astype(F32)
        gat[t][l, d] = acc.astype(BF16)
        for off in far_first:
            c_copy(t, l, off).start()

    def end_c(t, l):
        if D > 1:
            c_all(t, l).wait_recv()

    barrier = pltpu.get_barrier_semaphore()
    for off in range(1, D):
        pl.semaphore_signal(
            barrier, inc=1, device_id={"dom": lax.rem(d + off, D)}, device_id_type=MESH
        )
    for off in range(1, G):
        pl.semaphore_signal(
            barrier, inc=1, device_id={"group": lax.rem(g + off, G)}, device_id_type=MESH
        )

    def one_hot(row, ref, row0, height, col0):
        width = row.shape[1]
        sub = lax.broadcasted_iota(jnp.int16, (128, width), 0)
        for j in range(height // 128):
            at = (row - 128 * j).astype(jnp.int16)
            ref[row0 + j * 128 : row0 + (j + 1) * 128, col0 : col0 + width] = jnp.where(
                at == sub, BF16(1), BF16(0)
            )

    def spread(row):
        return jnp.broadcast_to(row, (128, row.shape[1])).T

    def one_hot_rows(ids, height, col0):
        lane = lax.broadcasted_iota(jnp.int16, (W, 128), 1)
        for i in range(E // W):
            at = spread(ids[:, i * W : (i + 1) * W]).astype(jnp.int16)
            for j in range(height // 128):
                oh[i * W : (i + 1) * W, col0 + j * 128 : col0 + (j + 1) * 128] = jnp.where(
                    at - jnp.int16(128 * j) == lane, BF16(1), BF16(0)
                )

    def halo_out(l, x_t):
        sent = mm(x_t, o_x[...]).astype(BF16)
        for k in range(4):
            fsrc[l, k] = sent[:, k * HALO : (k + 1) * HALO]

    for k in range(4):
        @pl.when(jnp.logical_not(in_ok[k]))
        def _(k=k):
            for l in range(L):
                tab_h[l, k] = jnp.zeros((H, HALO), BF16)

        @pl.when(jnp.logical_not(out_ok[k]))
        def _(k=k):
            for l in range(L):
                ret[l, k] = jnp.zeros((H, HALO), BF16)

    loads[0].wait()
    loads[1].wait()
    x_t = nodes[0].T
    tab[0] = x_t
    for k in range(4):
        one_hot(sidx[0, k : k + 1, :], o_x, 0, N, k * HALO)
    halo_out(0, x_t)
    pl.semaphore_wait(barrier, D - 1 + G - 1)
    send_halo(0)

    for load in loads[2:5]:
        load.wait()
    sids = snd[...]
    past = sids - N
    edge_0 = cnt[0, 0]
    edge_1 = edge_0 + cnt[0, 1]
    edge_2 = edge_1 + cnt[0, 2]
    sids = (
        sids
        + jnp.where(past >= edge_0, HALO - cnt[0, 0], 0)
        + jnp.where(past >= edge_1, HALO - cnt[0, 1], 0)
        + jnp.where(past >= edge_2, HALO - cnt[0, 2], 0)
    )
    rids = rcv[...]
    RQ, RS, RH = H, H + N, H + 2 * N
    TOP = RH + 4 * HALO
    one_hot(rids, rhs, RQ, N, 0)
    one_hot(sids, rhs, RS, N + 4 * HALO, 0)

    for load in loads[5:]:
        load.wait()
    first = edges[0].T
    stk[0, :H, :] = first
    rhs[:H, :] = first

    def column(row):
        return jnp.broadcast_to(row, (128, H)).T

    def centred(w, row):
        w = w.astype(F32)
        w = w - jnp.mean(w, axis=1, keepdims=True)
        col = column(row - jnp.mean(row, axis=1, keepdims=True))[:, :16]
        high = col.astype(BF16).astype(F32)
        mid = (col - high).astype(BF16).astype(F32)
        lane = lax.broadcasted_iota(jnp.int32, col.shape, 1)
        split = jnp.where(
            lane == 0,
            high,
            jnp.where(lane == 1, mid, jnp.where(lane == 2, col - high - mid, 0.0)),
        )
        return w.astype(BF16).T, split.astype(BF16)

    for l in range(L):
        for j in range(3):
            w1_t[l, j] = halved(w1[l, j * H : (j + 1) * H, :].T)
        w1_sq[l, :, :H] = w1[l, 2 * H :, :]
        w1_sq[l, :, H:] = w1[l, H : 2 * H, :]
        w2_t[l, :, :H], w2_t[l, :, H:] = centred(w2[l], bias[l, 1:2, :])
        w2_b[l] = halved(w2[l])
        n1_t[l] = halved(n1[l].T)
        n2_t[l, :, :H], n2_t[l, :, H:] = centred(n2[l], bias[l, 3:4, :])
        n2_b[l] = halved(n2[l])
        for j in range(2):
            cols[l, j] = column(bias[l, 2 * j : 2 * j + 1, :] * 0.5)
            cols[l, 2 + j] = column(gain[l, j : j + 1, :])

    def own_part(l):
        x_t = tab[l]
        own_l[:, :H] = w1_t[l, 0]
        own_l[:, H : H + N] = mm(w1_t[l, 2], x_t).astype(BF16)
        own_l[:, H + N :] = mm(w1_t[l, 1], x_t).astype(BF16)
        for i in range(E // W):
            part = slice(i * W, (i + 1) * W)
            slope[l, :, part] = mm(own_l[...], rhs[:RH, part]) + wide(cols[l, 0], W)

    for l in range(L):
        stk[l, H : H + 16, :] = jnp.ones((16, E), BF16)
        hid[l, H:, :] = jnp.ones((16, E), BF16)
        nhid[l, H:, :] = jnp.ones((16, N), BF16)
    one_hot_rows(rids, N, 0)

    def halo_rows(l):
        return jnp.concatenate([tab_h[l, k] for k in range(4)], axis=1)

    for l in range(L):
        own_part(l)
        if l == L - 1:
            if l > 0:
                halos = halo_rows(0)
                stk[0, H + 16 : 2 * H + 16, :] = (
                    mm(tab[0], rhs[RS:RH, :]) + mm(halos, rhs[RH:, :])
                ).astype(BF16)
                stk[0, 2 * H + 16 :, :] = mm(tab[0], rhs[RQ:RS, :]).astype(BF16)
            one_hot_rows(sids, N + 4 * HALO, N)
        wait_halo(l)
        if l == L - 1 and l == 0:
            halos = halo_rows(0)
            stk[0, H + 16 : 2 * H + 16, :] = (
                mm(tab[0], rhs[RS:RH, :]) + mm(halos, rhs[RH:, :])
            ).astype(BF16)
            stk[0, 2 * H + 16 :, :] = mm(tab[0], rhs[RQ:RS, :]).astype(BF16)
        for k in range(4):
            halo_l[:, k * HALO : (k + 1) * HALO] = mm(w1_t[l, 1], tab_h[l, k]).astype(BF16)

        def hidden(i, l=l):
            part = slice(i * W, (i + 1) * W)
            h_b, sl = silu_half(slope[l, :, part] + mm(halo_l[...], rhs[RH:, part]))
            hid[l, :H, part] = h_b
            slope[l, :, part] = sl

        def update(i, l=l):
            part = slice(i * W, (i + 1) * W)
            hat_c, inv_c = norm_parts(mm(w2_t[l], hid[l, :, part]))
            hat[l, :, part] = hat_c
            inv[l, :, part] = inv_c
            new = (stk[l, :H, part].astype(F32) + hat_c * wide(cols[l, 2], W)).astype(BF16)
            if l + 1 < L:
                stk[l + 1, :H, part] = new
                rhs[:H, part] = new
            else:
                e_last[:, part] = new

        for i in range(E // W):
            hidden(i)
        for i in range(E // W):
            update(i)

        x_t = tab[l]
        e_new = stk[l + 1, :H, :] if l + 1 < L else e_last[...]
        joined = jnp.concatenate([x_t, mm(e_new, oh[:, :N]).astype(BF16)], axis=0)
        jn[l] = joined
        h_b, sl = silu_half(mm(n1_t[l], joined) + wide(cols[l, 1], N))
        nhid[l, :H, :] = h_b
        nslope[l] = sl
        hat_c, inv_c = norm_parts(mm(n2_t[l], nhid[l]))
        nhat[l] = hat_c
        ninv[l] = inv_c
        x_new = (x_t.astype(F32) + hat_c * wide(cols[l, 3], N)).astype(BF16)
        if l + 1 < L:
            tab[l + 1] = x_new
            halo_out(l + 1, x_new)
            send_halo(l + 1)
        else:
            x_out[0] = x_new.T

    ones_n = jnp.ones((16, N), BF16)
    for l in reversed(range(L)):
        cot = ncot[0].T.astype(F32) if l == L - 1 else x_cot.astype(F32)
        dmn, nuh = norm_back(cot, wide(cols[l, 3], N), nhat[l], ninv[l])
        dmn = dmn.astype(BF16)
        dpn = (mm(n2_b[l], dmn) * nslope[l]).astype(BF16)
        djn = mm(n1[l], dpn)
        dx[...] = cot + djn[:H, :]
        dab = djn[H:, :].astype(BF16)

        def node_grads(l=l, dpn=dpn, dmn=dmn, nuh=nuh):
            one = mm_nt(jnp.concatenate([jn[l], ones_n], axis=0), dpn)
            two = mm_nt(nhid[l], dmn)
            start_a(
                0,
                l,
                [
                    one[: 2 * H],
                    two[:H],
                    one[2 * H : 2 * H + 1],
                    two[H : H + 1],
                    lane_sum(fold(nuh)) / gain[l, 1:2, :],
                ],
            )

        dge = jnp.zeros((H, 128), F32)

        def norm_cot(i, dge, l=l, dab=dab):
            part = slice(i * W, (i + 1) * W)
            c = mm(dab, rhs[RQ:RS, part])
            if l < L - 1:
                c = c + de[:, part].astype(F32)
            dm_c, uh_c = norm_back(c, wide(cols[l, 2], W), hat[l, :, part], inv[l, :, part])
            dm[:, part] = dm_c.astype(BF16)
            cc[:, part] = c
            return dge + fold(uh_c)

        def pre_cot(i, l=l):
            part = slice(i * W, (i + 1) * W)
            dp[:, part] = (mm(w2_b[l], dm[:, part]) * slope[l, :, part]).astype(BF16)

        for i in range(E // W):
            dge = norm_cot(i, dge)
            if l == 0 and i == 1:
                node_grads()
        for i in range(E // W):
            pre_cot(i)

        def halo_cots(l=l):
            u_h = mm(dp[...], oh[:, 2 * N :]).astype(BF16)
            for k in range(4):
                bsrc[l, k] = mm(
                    w1[l, H : 2 * H, :], u_h[:, k * HALO : (k + 1) * HALO]
                ).astype(BF16)
            send_ret(l)
            return u_h

        if l > 0:
            u_h = halo_cots()
            for i in range(E // W):
                part = slice(i * W, (i + 1) * W)
                de[:, part] = (cc[:, part] + mm(w1[l, :H, :], dp[:, part])).astype(BF16)
            u_o = mm(dp[...], oh[:, : 2 * N]).astype(BF16)
            one = mm_nt(stk[l, : H + 16, :], dp[...])
            two = mm_nt(hid[l], dm[...])
            w1_rows = [
                one[:H],
                mm_nt(tab[l], u_o[:, N:]) + mm_nt(halo_rows(l), u_h),
                mm_nt(tab[l], u_o[:, :N]),
            ]
            if l + 1 < L:
                start_b(0, l + 1)
                start_b(1, l + 1)
                start_c(0, l + 1)
                start_c(1, l + 1)
        else:
            one = mm_nt(stk[0], dp[...])
            two = mm_nt(hid[0], dm[...])
            start_a(
                1,
                0,
                [
                    one[:H],
                    one[H + 16 :],
                    two[:H],
                    one[H : H + 1],
                    two[H : H + 1],
                    lane_sum(dge) / gain[0, 0:1, :],
                ],
            )
            if L > 1:
                start_b(0, 1)
                start_b(1, 1)
            halo_cots()
            u_o = mm(dp[...], oh[:, : 2 * N]).astype(BF16)
        total = dx[...] + mm(
            w1_sq[l], jnp.concatenate([u_o[:, :N], u_o[:, N:]], axis=0)
        )
        if l > 0:
            start_a(
                1,
                l,
                w1_rows
                + [
                    two[:H],
                    one[H : H + 1],
                    two[H : H + 1],
                    lane_sum(dge) / gain[l, 0:1, :],
                ],
            )
            node_grads()
        else:
            for i in range(E // W):
                part = slice(i * W, (i + 1) * W)
                back = (cc[:, part] + mm(w1[l, :H, :], dp[:, part])).astype(BF16)
                e_grad[0, part, :] = back.T
            start_b(1, 0)
            start_b(0, 0)
            if L > 1:
                start_c(0, 1)
                start_c(1, 1)
        wait_ret(l)
        back_in = jnp.concatenate([ret[l, k] for k in range(4)], axis=1)
        x_cot = (total + mm_nt(back_in, o_x[...])).astype(BF16)
    x_grad[0] = x_cot.T

    for l in range(L):
        for k in range(4):
            @pl.when(out_ok[k])
            def _(k=k, l=l):
                fcopy(l, k).wait_send()

            @pl.when(in_ok[k])
            def _(k=k, l=l):
                bcopy(l, k).wait_send()
        for t in range(2):
            if D > 1:
                a_all(t, l).wait_send()
            if l > 0 and G > 1:
                b_all(t, l).wait_send()

    start_c(1, 0)
    start_c(0, 0)
    for t in range(2):
        if G > 1:
            b_all(t, 0).wait_send()
        for l in range(1, L):
            end_c(t, l)
            if D > 1:
                c_all(t, l).wait_send()
    for t in (1, 0):
        end_c(t, 0)
        if D > 1:
            c_all(t, 0).wait_send()


def finish(
    scale, H, x0, xg0, eg0, sum_n, sum_e,
    x1, xg1, eg1, g_w1, g_w2, g_n1, g_n2, g_b, g_g,
    v_w1, v_w2, v_n1, v_n2, v_b, v_g, sem,
):
    copies = [
        pltpu.make_async_copy(src, dst, sem.at[i])
        for i, (src, dst) in enumerate(((eg0, eg1), (x0, x1), (xg0, xg1)))
    ]
    for copy in copies:
        copy.start()
    L, D, share_n, _ = sum_n.shape
    share_e = sum_e.shape[2]
    for l in range(L):
        edge = (sum_e[l].astype(F32) * scale).reshape(D * share_e, H)
        v_w1[l] = edge[: 3 * H]
        v_w2[l] = edge[3 * H : 4 * H]
        edge = edge[4 * H : 4 * H + 8]
        v_b[l, 0:2, :] = edge[0:2]
        v_g[l, 0:1, :] = edge[2:3]
    copies.append(pltpu.make_async_copy(v_w1, g_w1, sem.at[3]))
    copies[-1].start()
    for l in range(L):
        node = (sum_n[l].astype(F32) * scale).reshape(D * share_n, H)
        v_n1[l] = node[: 2 * H]
        v_n2[l] = node[2 * H : 3 * H]
        node = node[3 * H : 3 * H + 8]
        v_b[l, 2:4, :] = node[0:2]
        v_g[l, 1:2, :] = node[2:3]
    for i, (src, dst) in enumerate(
        ((v_n1, g_n1), (v_n2, g_n2), (v_w2, g_w2), (v_b, g_b), (v_g, g_g))
    ):
        copies.append(pltpu.make_async_copy(src, dst, sem.at[4 + i]))
        copies[-1].start()
    for copy in copies:
        copy.wait()


def shards(D, G, nodes, edges, node_cot, send_index, halo_count, senders, receivers, *weights):
    edge_in_w, edge_out_w, node_in_w, node_out_w, biases, gains = weights
    _, N, H = nodes.shape
    E = edges.shape[1]
    L = edge_in_w.shape[0]
    HALO = send_index.shape[2]
    W = 256
    share_n = -(-(3 * H + 3) // (8 * D)) * 8
    share_e = -(-(4 * H + 3) // (8 * D)) * 8
    dims = (D, G, L, N, E, H, HALO, W, share_n, share_e)
    T = N + 4 * HALO
    own_shape = (
        pltpu.VMEM(nodes.shape, BF16),
        pltpu.VMEM(nodes.shape, BF16),
        pltpu.VMEM(edges.shape, BF16),
        pltpu.VMEM((L, D, share_n, H), BF16),
        pltpu.VMEM((L, D, share_e, H), BF16),
    )
    out_shape = (
        jax.ShapeDtypeStruct(nodes.shape, BF16),
        jax.ShapeDtypeStruct(nodes.shape, BF16),
        jax.ShapeDtypeStruct(edges.shape, BF16),
        jax.ShapeDtypeStruct(edge_in_w.shape, F32),
        jax.ShapeDtypeStruct(edge_out_w.shape, F32),
        jax.ShapeDtypeStruct(node_in_w.shape, F32),
        jax.ShapeDtypeStruct(node_out_w.shape, F32),
        jax.ShapeDtypeStruct(biases.shape, F32),
        jax.ShapeDtypeStruct(gains.shape, F32),
    )
    V = pltpu.VMEM
    dma = pltpu.SemaphoreType.DMA
    scratch = [
        V((H + N + T, E), BF16),
        V((N, 4 * HALO), BF16),
        V((H, H + 2 * N), BF16),
        V((H, 4 * HALO), BF16),
        V((L, H, N), BF16),
        V((L, 4, H, HALO), BF16),
        V((E, T + N), BF16),
        V((L, 3 * H + 16, E), BF16),
        V((H, E), BF16),
        V((L, H + 16, E), BF16),
        V((L, H, E), F32),
        V((L, H, E), F32),
        V((L, 1, E), F32),
        V((L, 2 * H, N), BF16),
        V((L, H + 16, N), BF16),
        V((L, H, N), F32),
        V((L, H, N), F32),
        V((L, 1, N), F32),
        V((L, 4, H, 128), F32),
        V((L, 3, H, H), BF16),
        V((L, H, 2 * H), BF16),
        V((L, H, H + 16), BF16),
        V((L, H, H), BF16),
        V((L, H, 2 * H), BF16),
        V((L, H, H + 16), BF16),
        V((L, H, H), BF16),
        V((H, E), BF16),
        V((H, E), BF16),
        V((H, E), F32),
        V((H, E), BF16),
        V((H, N), F32),
        V((L, 4, H, HALO), BF16),
        V((L, 4, H, HALO), BF16),
        V((L, 4, H, HALO), BF16),
        V((L, D, share_n, H), BF16),
        V((L, max(D - 1, 1), share_n, H), BF16),
        V((L, G, share_n, H), BF16),
        V((L, D, share_e, H), BF16),
        V((L, max(D - 1, 1), share_e, H), BF16),
        V((L, G, share_e, H), BF16),
        dma((L, 4)),
        dma((L, 4)),
        dma((L, 4)),
        dma((L, 4)),
        dma((2, L)),
        dma((2, L)),
        dma((2, L)),
        dma((2, L)),
        dma((2, L)),
        dma((2, L)),
        pltpu.SMEM(halo_count.shape, jnp.int32),
    ]
    operands = (nodes, edges, node_cot, send_index, senders, receivers) + weights
    scratch += [V(x.shape, x.dtype) for x in operands] + [dma((13,))]
    vm = pl.BlockSpec(memory_space=pltpu.VMEM)
    hbm = pl.BlockSpec(memory_space=pltpu.HBM)
    own = pl.pallas_call(
        functools.partial(kernel, dims),
        out_shape=own_shape,
        in_specs=[hbm] * 13,
        out_specs=tuple([vm] * 5),
        scratch_shapes=scratch,
        compiler_params=pltpu.CompilerParams(
            collective_id=0, has_side_effects=True, vmem_limit_bytes=VMEM_MAIN
        ),
    )(
        halo_count,
        *operands,
    )
    scale = (D * G * N) ** (-0.5)
    return pl.pallas_call(
        functools.partial(finish, scale, H),
        out_shape=out_shape,
        in_specs=[vm] * 5,
        out_specs=tuple([hbm] * 9),
        scratch_shapes=[V(x.shape, F32) for x in (edge_in_w, edge_out_w, node_in_w, node_out_w)]
        + [V(biases.shape, F32), V(gains.shape, F32), dma((9,))],
        compiler_params=pltpu.CompilerParams(vmem_limit_bytes=8 * 1024 * 1024),
    )(*own)


def solution(mesh):
    part3 = P(("dom", "group"), None, None)
    part2 = P(("dom", "group"), None)
    in_specs = (part3, part3, part3, part3, part2, part2, part2) + (P(),) * 6
    out_specs = (part3, part3, part3) + (P(),) * 6
    body = functools.partial(shards, mesh.shape["dom"], mesh.shape["group"])
    return jax.shard_map(
        body, mesh=mesh, in_specs=in_specs, out_specs=out_specs, check_vma=False
    )
```

```python
import functools

import jax
import jax.numpy as jnp
from jax import lax
from jax.experimental import pallas as pl
from jax.experimental.pallas import tpu as pltpu
from jax.sharding import PartitionSpec as P

F32 = jnp.float32
BF16 = jnp.bfloat16
MESH = pl.DeviceIdType.MESH
VMEM_MAIN = 58 * 1024 * 1024


def mm(a, b):
    return lax.dot_general(a, b, (((1,), (0,)), ((), ())), preferred_element_type=F32)


def mm_nt(a, b):
    return lax.dot_general(a, b, (((1,), (1,)), ((), ())), preferred_element_type=F32)


def norm_parts(values):
    spread = jnp.mean(values * values, axis=0, keepdims=True)
    inv = lax.rsqrt(spread + 1e-05)
    return values * inv, inv


def norm_back(cot, gain_col, hat, inv):
    u = cot * gain_col
    uh = u * hat
    back = inv * (
        u
        - jnp.mean(u, axis=0, keepdims=True)
        - hat * jnp.mean(uh, axis=0, keepdims=True)
    )
    return back, uh


def fold(x):
    total = x[:, :128]
    for i in range(1, x.shape[1] // 128):
        total = total + x[:, i * 128 : (i + 1) * 128]
    return total


def lane_sum(x):
    return jnp.sum(x.T, axis=0, keepdims=True)


def silu_half(half):
    t = jnp.tanh(half)
    a = 1.0 + t
    h = half * a
    return h.astype(BF16), a + h * (1.0 - t)


def halved(x):
    return (x.astype(F32) * 0.5).astype(BF16)


def wide(tile, width):
    return jnp.concatenate([tile] * (width // tile.shape[1]), axis=1)


def kernel(
    dims,
    cnt_h,
    nodes_h,
    edges_h,
    ncot_h,
    sidx_h,
    snd_h,
    rcv_h,
    w1_h,
    w2_h,
    n1_h,
    n2_h,
    bias_h,
    gain_h,
    x_out,
    x_grad,
    e_grad,
    sum_n,
    sum_e,
    rhs,
    o_x,
    own_l,
    halo_l,
    tab,
    tab_h,
    oh,
    stk,
    e_last,
    hid,
    slope,
    hat,
    inv,
    jn,
    nhid,
    nslope,
    nhat,
    ninv,
    cols,
    w1_t,
    w1_sq,
    w2_t,
    w2_b,
    n1_t,
    n2_t,
    n2_b,
    dm,
    dp,
    cc,
    de,
    dx,
    fsrc,
    bsrc,
    ret,
    grads_n,
    buf_an,
    buf_bn,
    grads_e,
    buf_ae,
    buf_be,
    fs,
    fr,
    bs,
    br,
    a_s,
    a_r,
    b_s,
    b_r,
    c_s,
    c_r,
    cnt,
    nodes,
    edges,
    ncot,
    sidx,
    snd,
    rcv,
    w1,
    w2,
    n1,
    n2,
    bias,
    gain,
    in_sem,
    met,
):
    D, G, L, N, E, H, HALO, W, share_n, share_e = dims
    shares = (share_n, share_e)
    grads = (grads_n, grads_e)
    buf_a = (buf_an, buf_ae)
    buf_b = (buf_bn, buf_be)
    gat = (sum_n, sum_e)
    loads = [
        pltpu.make_async_copy(src, dst, in_sem.at[i])
        for i, (src, dst) in enumerate(
            (
                (nodes_h, nodes),
                (sidx_h, sidx),
                (snd_h, snd),
                (rcv_h, rcv),
                (cnt_h, cnt),
                (edges_h, edges),
                (w1_h, w1),
                (w2_h, w2),
                (bias_h, bias),
                (gain_h, gain),
                (n1_h, n1),
                (n2_h, n2),
                (ncot_h, ncot),
            )
        )
    ]
    for load in loads:
        load.start()
    d = lax.axis_index("dom")
    g = lax.axis_index("group")

    has_up = d + 1 < D
    has_down = d > 0
    has_right = g + 1 < G
    has_left = g > 0
    out_ok = (has_up, has_down, has_right, has_left)
    in_ok = (has_down, has_up, has_left, has_right)
    out_dev = ({"dom": d + 1}, {"dom": d - 1}, {"group": g + 1}, {"group": g - 1})
    in_dev = ({"dom": d - 1}, {"dom": d + 1}, {"group": g - 1}, {"group": g + 1})

    def fcopy(l, k):
        return pltpu.make_async_remote_copy(
            src_ref=fsrc.at[l, k],
            dst_ref=tab_h.at[l, k],
            send_sem=fs.at[l, k],
            recv_sem=fr.at[l, k],
            device_id=out_dev[k],
            device_id_type=MESH,
        )

    def bcopy(l, k):
        return pltpu.make_async_remote_copy(
            src_ref=bsrc.at[l, k],
            dst_ref=ret.at[l, k],
            send_sem=bs.at[l, k],
            recv_sem=br.at[l, k],
            device_id=in_dev[k],
            device_id_type=MESH,
        )

    def send_halo(l):
        for k in range(4):
            @pl.when(out_ok[k])
            def _(k=k):
                fcopy(l, k).start()

    def wait_halo(l):
        for k in range(4):
            @pl.when(in_ok[k])
            def _(k=k):
                fcopy(l, k).wait_recv()

    def send_ret(l):
        for k in range(4):
            @pl.when(in_ok[k])
            def _(k=k):
                bcopy(l, k).start()

    def wait_ret(l):
        for k in range(4):
            @pl.when(out_ok[k])
            def _(k=k):
                bcopy(l, k).wait_recv()

    far_first = sorted(range(1, D), key=lambda off: abs(2 * off - D))

    def a_copy(t, l, off):
        peer = lax.rem(d + off, D)
        return pltpu.make_async_remote_copy(
            src_ref=grads[t].at[l, peer],
            dst_ref=buf_a[t].at[l, off - 1],
            send_sem=a_s.at[t, l],
            recv_sem=a_r.at[t, l],
            device_id={"dom": peer},
            device_id_type=MESH,
        )

    def b_copy(t, l, off):
        return pltpu.make_async_remote_copy(
            src_ref=buf_b[t].at[l, g],
            dst_ref=buf_b[t].at[l, g],
            send_sem=b_s.at[t, l],
            recv_sem=b_r.at[t, l],
            device_id={"group": lax.rem(g + off, G)},
            device_id_type=MESH,
        )

    def c_copy(t, l, off):
        return pltpu.make_async_remote_copy(
            src_ref=gat[t].at[l, d],
            dst_ref=gat[t].at[l, d],
            send_sem=c_s.at[t, l],
            recv_sem=c_r.at[t, l],
            device_id={"dom": lax.rem(d + off, D)},
            device_id_type=MESH,
        )

    def every(ref, send_sem, recv_sem, axis, here, size):
        return pltpu.make_async_remote_copy(
            src_ref=ref,
            dst_ref=ref,
            send_sem=send_sem,
            recv_sem=recv_sem,
            device_id={axis: lax.rem(here + 1, size)},
            device_id_type=MESH,
        )

    def a_all(t, l):
        return every(buf_a[t].at[l, pl.ds(0, D - 1)], a_s.at[t, l], a_r.at[t, l], "dom", d, D)

    def b_all(t, l):
        return every(buf_b[t].at[l, pl.ds(0, G - 1)], b_s.at[t, l], b_r.at[t, l], "group", g, G)

    def c_all(t, l):
        return every(gat[t].at[l, pl.ds(0, D - 1)], c_s.at[t, l], c_r.at[t, l], "dom", d, D)

    def start_a(t, l, pieces):
        rows = sum(p.shape[0] for p in pieces)
        pad = jnp.zeros((D * shares[t] - rows, H), F32)
        whole = jnp.concatenate(list(pieces) + [pad], axis=0)
        grads[t][l] = whole.reshape(D, shares[t], H).astype(BF16)
        for off in far_first:
            a_copy(t, l, off).start()

    def start_b(t, l):
        if D > 1:
            a_all(t, l).wait_recv()
        acc = grads[t][l, d].astype(F32)
        for off in range(1, D):
            acc = acc + buf_a[t][l, off - 1].astype(F32)
        buf_b[t][l, g] = acc.astype(BF16)
        for off in range(1, G):
            b_copy(t, l, off).start()

    def start_c(t, l):
        if G > 1:
            b_all(t, l).wait_recv()
        acc = buf_b[t][l, 0].astype(F32)
        for i in range(1, G):
            acc = acc + buf_b[t][l, i].astype(F32)
        gat[t][l, d] = acc.astype(BF16)
        for off in far_first:
            c_copy(t, l, off).start()

    def end_c(t, l):
        if D > 1:
            c_all(t, l).wait_recv()

    barrier = pltpu.get_barrier_semaphore()
    for k in range(4):
        @pl.when(out_ok[k])
        def _(k=k):
            pl.semaphore_signal(barrier, inc=1, device_id=out_dev[k], device_id_type=MESH)

    def count(*flags):
        return sum(jnp.where(flag, 1, 0) for flag in flags)

    steps = [
        (off, [("dom", d, D)] * (off < D - 1) + [("group", g, G)] * (off < G - 1))
        for off in (2**i for i in range(max(D, G).bit_length()))
        if off < max(D, G) - 1
    ]

    def greet(i):
        off, axes = steps[i]
        for axis, here, size in axes:
            @pl.when(here + off < size)
            def _(axis=axis, here=here, off=off):
                pl.semaphore_signal(
                    met.at[i], inc=1, device_id={axis: here + off}, device_id_type=MESH
                )

            @pl.when(here >= off)
            def _(axis=axis, here=here, off=off):
                pl.semaphore_signal(
                    met.at[i], inc=1, device_id={axis: here - off}, device_id_type=MESH
                )

    def greeted(i):
        off, axes = steps[i]
        pl.semaphore_wait(
            met.at[i],
            count(
                *[here + off < size for _, here, size in axes],
                *[here >= off for _, here, _ in axes],
            ),
        )

    def one_hot(row, ref, row0, height, col0):
        width = row.shape[1]
        sub = lax.broadcasted_iota(jnp.int16, (128, width), 0)
        for j in range(height // 128):
            at = (row - 128 * j).astype(jnp.int16)
            ref[row0 + j * 128 : row0 + (j + 1) * 128, col0 : col0 + width] = jnp.where(
                at == sub, BF16(1), BF16(0)
            )

    def spread(row):
        return jnp.broadcast_to(row, (128, row.shape[1])).T

    def one_hot_rows(ids, height, col0):
        lane = lax.broadcasted_iota(jnp.int16, (W, 128), 1)
        for i in range(E // W):
            at = spread(ids[:, i * W : (i + 1) * W]).astype(jnp.int16)
            for j in range(height // 128):
                oh[i * W : (i + 1) * W, col0 + j * 128 : col0 + (j + 1) * 128] = jnp.where(
                    at - jnp.int16(128 * j) == lane, BF16(1), BF16(0)
                )

    def halo_out(l, x_t):
        sent = mm(x_t, o_x[...]).astype(BF16)
        for k in range(4):
            fsrc[l, k] = sent[:, k * HALO : (k + 1) * HALO]

    for k in range(4):
        @pl.when(jnp.logical_not(in_ok[k]))
        def _(k=k):
            for l in range(L):
                tab_h[l, k] = jnp.zeros((H, HALO), BF16)

        @pl.when(jnp.logical_not(out_ok[k]))
        def _(k=k):
            for l in range(L):
                ret[l, k] = jnp.zeros((H, HALO), BF16)

    loads[0].wait()
    loads[1].wait()
    x_t = nodes[0].T
    tab[0] = x_t
    for k in range(4):
        one_hot(sidx[0, k : k + 1, :], o_x, 0, N, k * HALO)
    halo_out(0, x_t)
    pl.semaphore_wait(barrier, count(*out_ok))
    send_halo(0)
    if steps:
        greet(0)

    for load in loads[2:5]:
        load.wait()
    sids = snd[...]
    past = sids - N
    edge_0 = cnt[0, 0]
    edge_1 = edge_0 + cnt[0, 1]
    edge_2 = edge_1 + cnt[0, 2]
    sids = (
        sids
        + jnp.where(past >= edge_0, HALO - cnt[0, 0], 0)
        + jnp.where(past >= edge_1, HALO - cnt[0, 1], 0)
        + jnp.where(past >= edge_2, HALO - cnt[0, 2], 0)
    )
    rids = rcv[...]
    RQ, RS, RH = H, H + N, H + 2 * N
    TOP = RH + 4 * HALO
    one_hot(rids, rhs, RQ, N, 0)
    one_hot(sids, rhs, RS, N + 4 * HALO, 0)

    for load in loads[5:]:
        load.wait()
    first = edges[0].T
    stk[0, :H, :] = first
    rhs[:H, :] = first

    def column(row):
        return jnp.broadcast_to(row, (128, H)).T

    def centred(w, row):
        w = w.astype(F32)
        w = w - jnp.mean(w, axis=1, keepdims=True)
        col = column(row - jnp.mean(row, axis=1, keepdims=True))[:, :16]
        high = col.astype(BF16).astype(F32)
        mid = (col - high).astype(BF16).astype(F32)
        lane = lax.broadcasted_iota(jnp.int32, col.shape, 1)
        split = jnp.where(
            lane == 0,
            high,
            jnp.where(lane == 1, mid, jnp.where(lane == 2, col - high - mid, 0.0)),
        )
        return w.astype(BF16).T, split.astype(BF16)

    for l in range(L):
        for j in range(3):
            w1_t[l, j] = halved(w1[l, j * H : (j + 1) * H, :].T)
        w1_sq[l, :, :H] = w1[l, 2 * H :, :]
        w1_sq[l, :, H:] = w1[l, H : 2 * H, :]
        w2_t[l, :, :H], w2_t[l, :, H:] = centred(w2[l], bias[l, 1:2, :])
        w2_b[l] = halved(w2[l])
        n1_t[l] = halved(n1[l].T)
        n2_t[l, :, :H], n2_t[l, :, H:] = centred(n2[l], bias[l, 3:4, :])
        n2_b[l] = halved(n2[l])
        for j in range(2):
            cols[l, j] = column(bias[l, 2 * j : 2 * j + 1, :] * 0.5)
            cols[l, 2 + j] = column(gain[l, j : j + 1, :])

    def own_part(l):
        x_t = tab[l]
        own_l[:, :H] = w1_t[l, 0]
        own_l[:, H : H + N] = mm(w1_t[l, 2], x_t).astype(BF16)
        own_l[:, H + N :] = mm(w1_t[l, 1], x_t).astype(BF16)
        for i in range(E // W):
            part = slice(i * W, (i + 1) * W)
            slope[l, :, part] = mm(own_l[...], rhs[:RH, part]) + wide(cols[l, 0], W)

    for l in range(L):
        stk[l, H : H + 16, :] = jnp.ones((16, E), BF16)
        hid[l, H:, :] = jnp.ones((16, E), BF16)
        nhid[l, H:, :] = jnp.ones((16, N), BF16)
    one_hot_rows(rids, N, 0)

    def halo_rows(l):
        return jnp.concatenate([tab_h[l, k] for k in range(4)], axis=1)

    for l in range(L):
        own_part(l)
        if l == 0 and len(steps) > 1:
            greeted(0)
            greet(1)
        if l == L - 1:
            if l > 0:
                halos = halo_rows(0)
                stk[0, H + 16 : 2 * H + 16, :] = (
                    mm(tab[0], rhs[RS:RH, :]) + mm(halos, rhs[RH:, :])
                ).astype(BF16)
                stk[0, 2 * H + 16 :, :] = mm(tab[0], rhs[RQ:RS, :]).astype(BF16)
            one_hot_rows(sids, N + 4 * HALO, N)
            for i in range(2, len(steps)):
                greeted(i - 1)
                greet(i)
        wait_halo(l)
        if l == L - 1 and l == 0:
            halos = halo_rows(0)
            stk[0, H + 16 : 2 * H + 16, :] = (
                mm(tab[0], rhs[RS:RH, :]) + mm(halos, rhs[RH:, :])
            ).astype(BF16)
            stk[0, 2 * H + 16 :, :] = mm(tab[0], rhs[RQ:RS, :]).astype(BF16)
        for k in range(4):
            halo_l[:, k * HALO : (k + 1) * HALO] = mm(w1_t[l, 1], tab_h[l, k]).astype(BF16)

        def hidden(i, l=l):
            part = slice(i * W, (i + 1) * W)
            h_b, sl = silu_half(slope[l, :, part] + mm(halo_l[...], rhs[RH:, part]))
            hid[l, :H, part] = h_b
            slope[l, :, part] = sl

        def update(i, l=l):
            part = slice(i * W, (i + 1) * W)
            hat_c, inv_c = norm_parts(mm(w2_t[l], hid[l, :, part]))
            hat[l, :, part] = hat_c
            inv[l, :, part] = inv_c
            new = (stk[l, :H, part].astype(F32) + hat_c * wide(cols[l, 2], W)).astype(BF16)
            if l + 1 < L:
                stk[l + 1, :H, part] = new
                rhs[:H, part] = new
            else:
                e_last[:, part] = new

        for i in range(E // W):
            hidden(i)
        for i in range(E // W):
            update(i)

        x_t = tab[l]
        e_new = stk[l + 1, :H, :] if l + 1 < L else e_last[...]
        joined = jnp.concatenate([x_t, mm(e_new, oh[:, :N]).astype(BF16)], axis=0)
        jn[l] = joined
        h_b, sl = silu_half(mm(n1_t[l], joined) + wide(cols[l, 1], N))
        nhid[l, :H, :] = h_b
        nslope[l] = sl
        hat_c, inv_c = norm_parts(mm(n2_t[l], nhid[l]))
        nhat[l] = hat_c
        ninv[l] = inv_c
        x_new = (x_t.astype(F32) + hat_c * wide(cols[l, 3], N)).astype(BF16)
        if l + 1 < L:
            tab[l + 1] = x_new
            halo_out(l + 1, x_new)
            send_halo(l + 1)
        else:
            x_out[0] = x_new.T

    ones_n = jnp.ones((16, N), BF16)
    for l in reversed(range(L)):
        cot = ncot[0].T.astype(F32) if l == L - 1 else x_cot.astype(F32)
        dmn, nuh = norm_back(cot, wide(cols[l, 3], N), nhat[l], ninv[l])
        dmn = dmn.astype(BF16)
        dpn = (mm(n2_b[l], dmn) * nslope[l]).astype(BF16)
        djn = mm(n1[l], dpn)
        dx[...] = cot + djn[:H, :]
        dab = djn[H:, :].astype(BF16)

        def node_grads(l=l, dpn=dpn, dmn=dmn, nuh=nuh):
            one = mm_nt(jnp.concatenate([jn[l], ones_n], axis=0), dpn)
            two = mm_nt(nhid[l], dmn)
            start_a(
                0,
                l,
                [
                    one[: 2 * H],
                    two[:H],
                    one[2 * H : 2 * H + 1],
                    two[H : H + 1],
                    lane_sum(fold(nuh)) / gain[l, 1:2, :],
                ],
            )

        dge = jnp.zeros((H, 128), F32)

        def norm_cot(i, dge, l=l, dab=dab):
            part = slice(i * W, (i + 1) * W)
            c = mm(dab, rhs[RQ:RS, part])
            if l < L - 1:
                c = c + de[:, part].astype(F32)
            dm_c, uh_c = norm_back(c, wide(cols[l, 2], W), hat[l, :, part], inv[l, :, part])
            dm[:, part] = dm_c.astype(BF16)
            cc[:, part] = c
            return dge + fold(uh_c)

        def pre_cot(i, l=l):
            part = slice(i * W, (i + 1) * W)
            dp[:, part] = (mm(w2_b[l], dm[:, part]) * slope[l, :, part]).astype(BF16)

        for i in range(E // W):
            dge = norm_cot(i, dge)
            if l == 0 and i == 1:
                node_grads()
        for i in range(E // W):
            pre_cot(i)

        def halo_cots(l=l):
            u_h = mm(dp[...], oh[:, 2 * N :]).astype(BF16)
            for k in range(4):
                bsrc[l, k] = mm(
                    w1[l, H : 2 * H, :], u_h[:, k * HALO : (k + 1) * HALO]
                ).astype(BF16)
            send_ret(l)
            return u_h

        if l > 0:
            u_h = halo_cots()
            for i in range(E // W):
                part = slice(i * W, (i + 1) * W)
                de[:, part] = (cc[:, part] + mm(w1[l, :H, :], dp[:, part])).astype(BF16)
            u_o = mm(dp[...], oh[:, : 2 * N]).astype(BF16)
            one = mm_nt(stk[l, : H + 16, :], dp[...])
            two = mm_nt(hid[l], dm[...])
            w1_rows = [
                one[:H],
                mm_nt(tab[l], u_o[:, N:]) + mm_nt(halo_rows(l), u_h),
                mm_nt(tab[l], u_o[:, :N]),
            ]
            if l + 1 < L:
                start_b(0, l + 1)
                start_b(1, l + 1)
                start_c(0, l + 1)
                start_c(1, l + 1)
        else:
            one = mm_nt(stk[0], dp[...])
            two = mm_nt(hid[0], dm[...])
            start_a(
                1,
                0,
                [
                    one[:H],
                    one[H + 16 :],
                    two[:H],
                    one[H : H + 1],
                    two[H : H + 1],
                    lane_sum(dge) / gain[0, 0:1, :],
                ],
            )
            if L > 1:
                start_b(0, 1)
                start_b(1, 1)
            halo_cots()
            u_o = mm(dp[...], oh[:, : 2 * N]).astype(BF16)
        total = dx[...] + mm(
            w1_sq[l], jnp.concatenate([u_o[:, :N], u_o[:, N:]], axis=0)
        )
        if l > 0:
            if l == L - 1 and steps:
                greeted(len(steps) - 1)
            start_a(
                1,
                l,
                w1_rows
                + [
                    two[:H],
                    one[H : H + 1],
                    two[H : H + 1],
                    lane_sum(dge) / gain[l, 0:1, :],
                ],
            )
            node_grads()
        else:
            for i in range(E // W):
                part = slice(i * W, (i + 1) * W)
                back = (cc[:, part] + mm(w1[l, :H, :], dp[:, part])).astype(BF16)
                e_grad[0, part, :] = back.T
            start_b(1, 0)
            start_b(0, 0)
            if L > 1:
                start_c(0, 1)
                start_c(1, 1)
        wait_ret(l)
        back_in = jnp.concatenate([ret[l, k] for k in range(4)], axis=1)
        x_cot = (total + mm_nt(back_in, o_x[...])).astype(BF16)
    x_grad[0] = x_cot.T

    for l in range(L):
        for k in range(4):
            @pl.when(out_ok[k])
            def _(k=k, l=l):
                fcopy(l, k).wait_send()

            @pl.when(in_ok[k])
            def _(k=k, l=l):
                bcopy(l, k).wait_send()
        for t in range(2):
            if D > 1:
                a_all(t, l).wait_send()
            if l > 0 and G > 1:
                b_all(t, l).wait_send()

    start_c(1, 0)
    start_c(0, 0)
    for t in range(2):
        if G > 1:
            b_all(t, 0).wait_send()
        for l in range(1, L):
            end_c(t, l)
            if D > 1:
                c_all(t, l).wait_send()
    for t in (1, 0):
        end_c(t, 0)
        if D > 1:
            c_all(t, 0).wait_send()


def finish(
    scale, H, x0, xg0, eg0, sum_n, sum_e,
    x1, xg1, eg1, g_w1, g_w2, g_n1, g_n2, g_b, g_g,
    v_w1, v_w2, v_n1, v_n2, v_b, v_g, sem,
):
    copies = [
        pltpu.make_async_copy(src, dst, sem.at[i])
        for i, (src, dst) in enumerate(((eg0, eg1), (x0, x1), (xg0, xg1)))
    ]
    for copy in copies:
        copy.start()
    L, D, share_n, _ = sum_n.shape
    share_e = sum_e.shape[2]
    for l in range(L):
        edge = (sum_e[l].astype(F32) * scale).reshape(D * share_e, H)
        v_w1[l] = edge[: 3 * H]
        v_w2[l] = edge[3 * H : 4 * H]
        edge = edge[4 * H : 4 * H + 8]
        v_b[l, 0:2, :] = edge[0:2]
        v_g[l, 0:1, :] = edge[2:3]
    copies.append(pltpu.make_async_copy(v_w1, g_w1, sem.at[3]))
    copies[-1].start()
    for l in range(L):
        node = (sum_n[l].astype(F32) * scale).reshape(D * share_n, H)
        v_n1[l] = node[: 2 * H]
        v_n2[l] = node[2 * H : 3 * H]
        node = node[3 * H : 3 * H + 8]
        v_b[l, 2:4, :] = node[0:2]
        v_g[l, 1:2, :] = node[2:3]
    for i, (src, dst) in enumerate(
        ((v_n1, g_n1), (v_n2, g_n2), (v_w2, g_w2), (v_b, g_b), (v_g, g_g))
    ):
        copies.append(pltpu.make_async_copy(src, dst, sem.at[4 + i]))
        copies[-1].start()
    for copy in copies:
        copy.wait()


def shards(D, G, nodes, edges, node_cot, send_index, halo_count, senders, receivers, *weights):
    edge_in_w, edge_out_w, node_in_w, node_out_w, biases, gains = weights
    _, N, H = nodes.shape
    E = edges.shape[1]
    L = edge_in_w.shape[0]
    HALO = send_index.shape[2]
    W = 256
    share_n = -(-(3 * H + 3) // (8 * D)) * 8
    share_e = -(-(4 * H + 3) // (8 * D)) * 8
    dims = (D, G, L, N, E, H, HALO, W, share_n, share_e)
    T = N + 4 * HALO
    own_shape = (
        pltpu.VMEM(nodes.shape, BF16),
        pltpu.VMEM(nodes.shape, BF16),
        pltpu.VMEM(edges.shape, BF16),
        pltpu.VMEM((L, D, share_n, H), BF16),
        pltpu.VMEM((L, D, share_e, H), BF16),
    )
    out_shape = (
        jax.ShapeDtypeStruct(nodes.shape, BF16),
        jax.ShapeDtypeStruct(nodes.shape, BF16),
        jax.ShapeDtypeStruct(edges.shape, BF16),
        jax.ShapeDtypeStruct(edge_in_w.shape, F32),
        jax.ShapeDtypeStruct(edge_out_w.shape, F32),
        jax.ShapeDtypeStruct(node_in_w.shape, F32),
        jax.ShapeDtypeStruct(node_out_w.shape, F32),
        jax.ShapeDtypeStruct(biases.shape, F32),
        jax.ShapeDtypeStruct(gains.shape, F32),
    )
    V = pltpu.VMEM
    dma = pltpu.SemaphoreType.DMA
    scratch = [
        V((H + N + T, E), BF16),
        V((N, 4 * HALO), BF16),
        V((H, H + 2 * N), BF16),
        V((H, 4 * HALO), BF16),
        V((L, H, N), BF16),
        V((L, 4, H, HALO), BF16),
        V((E, T + N), BF16),
        V((L, 3 * H + 16, E), BF16),
        V((H, E), BF16),
        V((L, H + 16, E), BF16),
        V((L, H, E), F32),
        V((L, H, E), F32),
        V((L, 1, E), F32),
        V((L, 2 * H, N), BF16),
        V((L, H + 16, N), BF16),
        V((L, H, N), F32),
        V((L, H, N), F32),
        V((L, 1, N), F32),
        V((L, 4, H, 128), F32),
        V((L, 3, H, H), BF16),
        V((L, H, 2 * H), BF16),
        V((L, H, H + 16), BF16),
        V((L, H, H), BF16),
        V((L, H, 2 * H), BF16),
        V((L, H, H + 16), BF16),
        V((L, H, H), BF16),
        V((H, E), BF16),
        V((H, E), BF16),
        V((H, E), F32),
        V((H, E), BF16),
        V((H, N), F32),
        V((L, 4, H, HALO), BF16),
        V((L, 4, H, HALO), BF16),
        V((L, 4, H, HALO), BF16),
        V((L, D, share_n, H), BF16),
        V((L, max(D - 1, 1), share_n, H), BF16),
        V((L, G, share_n, H), BF16),
        V((L, D, share_e, H), BF16),
        V((L, max(D - 1, 1), share_e, H), BF16),
        V((L, G, share_e, H), BF16),
        dma((L, 4)),
        dma((L, 4)),
        dma((L, 4)),
        dma((L, 4)),
        dma((2, L)),
        dma((2, L)),
        dma((2, L)),
        dma((2, L)),
        dma((2, L)),
        dma((2, L)),
        pltpu.SMEM(halo_count.shape, jnp.int32),
    ]
    operands = (nodes, edges, node_cot, send_index, senders, receivers) + weights
    scratch += [V(x.shape, x.dtype) for x in operands] + [dma((13,)), pltpu.SemaphoreType.REGULAR((max(D, G).bit_length(),))]
    vm = pl.BlockSpec(memory_space=pltpu.VMEM)
    hbm = pl.BlockSpec(memory_space=pltpu.HBM)
    own = pl.pallas_call(
        functools.partial(kernel, dims),
        out_shape=own_shape,
        in_specs=[hbm] * 13,
        out_specs=tuple([vm] * 5),
        scratch_shapes=scratch,
        compiler_params=pltpu.CompilerParams(
            collective_id=0, has_side_effects=True, vmem_limit_bytes=VMEM_MAIN
        ),
    )(
        halo_count,
        *operands,
    )
    scale = (D * G * N) ** (-0.5)
    return pl.pallas_call(
        functools.partial(finish, scale, H),
        out_shape=out_shape,
        in_specs=[vm] * 5,
        out_specs=tuple([hbm] * 9),
        scratch_shapes=[V(x.shape, F32) for x in (edge_in_w, edge_out_w, node_in_w, node_out_w)]
        + [V(biases.shape, F32), V(gains.shape, F32), dma((9,))],
        compiler_params=pltpu.CompilerParams(vmem_limit_bytes=8 * 1024 * 1024),
    )(*own)


def solution(mesh):
    part3 = P(("dom", "group"), None, None)
    part2 = P(("dom", "group"), None)
    in_specs = (part3, part3, part3, part3, part2, part2, part2) + (P(),) * 6
    out_specs = (part3, part3, part3) + (P(),) * 6
    body = functools.partial(shards, mesh.shape["dom"], mesh.shape["group"])
    return jax.shard_map(
        body, mesh=mesh, in_specs=in_specs, out_specs=out_specs, check_vma=False
    )
```

```python
import functools

import jax
import jax.numpy as jnp
from jax import lax
from jax.experimental import pallas as pl
from jax.experimental.pallas import tpu as pltpu
from jax.sharding import PartitionSpec as P

F32 = jnp.float32
BF16 = jnp.bfloat16
MESH = pl.DeviceIdType.MESH
VMEM_MAIN = 58 * 1024 * 1024


def mm(a, b):
    return lax.dot_general(a, b, (((1,), (0,)), ((), ())), preferred_element_type=F32)


def mm_nt(a, b):
    return lax.dot_general(a, b, (((1,), (1,)), ((), ())), preferred_element_type=F32)


def norm_parts(values):
    spread = jnp.mean(values * values, axis=0, keepdims=True)
    inv = lax.rsqrt(spread + 1e-05)
    return values * inv, inv


def norm_back(cot, gain_col, hat, inv):
    u = cot * gain_col
    uh = u * hat
    back = inv * (
        u
        - jnp.mean(u, axis=0, keepdims=True)
        - hat * jnp.mean(uh, axis=0, keepdims=True)
    )
    return back, uh


def fold(x):
    total = x[:, :128]
    for i in range(1, x.shape[1] // 128):
        total = total + x[:, i * 128 : (i + 1) * 128]
    return total


def lane_sum(x):
    return jnp.sum(x.T, axis=0, keepdims=True)


def silu_half(half):
    t = jnp.tanh(half)
    a = 1.0 + t
    h = half * a
    return h.astype(BF16), a + h * (1.0 - t)


def halved(x):
    return (x.astype(F32) * 0.5).astype(BF16)


def wide(tile, width):
    return jnp.concatenate([tile] * (width // tile.shape[1]), axis=1)


def kernel(
    dims,
    cnt_h,
    nodes_h,
    edges_h,
    ncot_h,
    sidx_h,
    snd_h,
    rcv_h,
    w1_h,
    w2_h,
    n1_h,
    n2_h,
    bias_h,
    gain_h,
    x_out,
    x_grad,
    e_grad,
    sum_n,
    sum_e,
    rhs,
    o_x,
    own_l,
    halo_l,
    tab,
    tab_h,
    oh,
    stk,
    e_last,
    hid,
    slope,
    hat,
    inv,
    jn,
    nhid,
    nslope,
    nhat,
    ninv,
    cols,
    w1_t,
    w1_sq,
    w2_t,
    w2_b,
    n1_t,
    n2_t,
    n2_b,
    dm,
    dp,
    cc,
    de,
    dx,
    fsrc,
    bsrc,
    ret,
    grads_n,
    buf_an,
    buf_bn,
    grads_e,
    buf_ae,
    buf_be,
    fs,
    fr,
    bs,
    br,
    a_s,
    a_r,
    b_s,
    b_r,
    c_s,
    c_r,
    cnt,
    nodes,
    edges,
    ncot,
    sidx,
    snd,
    rcv,
    w1,
    w2,
    n1,
    n2,
    bias,
    gain,
    in_sem,
    met,
):
    D, G, L, N, E, H, HALO, W, share_n, share_e = dims
    shares = (share_n, share_e)
    grads = (grads_n, grads_e)
    buf_a = (buf_an, buf_ae)
    buf_b = (buf_bn, buf_be)
    gat = (sum_n, sum_e)
    loads = [
        pltpu.make_async_copy(src, dst, in_sem.at[i])
        for i, (src, dst) in enumerate(
            (
                (nodes_h, nodes),
                (sidx_h, sidx),
                (snd_h, snd),
                (rcv_h, rcv),
                (cnt_h, cnt),
                (edges_h, edges),
                (w1_h, w1),
                (w2_h, w2),
                (bias_h, bias),
                (gain_h, gain),
                (n1_h, n1),
                (n2_h, n2),
                (ncot_h, ncot),
            )
        )
    ]
    for load in loads:
        load.start()
    d = lax.axis_index("dom")
    g = lax.axis_index("group")

    has_up = d + 1 < D
    has_down = d > 0
    has_right = g + 1 < G
    has_left = g > 0
    out_ok = (has_up, has_down, has_right, has_left)
    in_ok = (has_down, has_up, has_left, has_right)
    out_dev = ({"dom": d + 1}, {"dom": d - 1}, {"group": g + 1}, {"group": g - 1})
    in_dev = ({"dom": d - 1}, {"dom": d + 1}, {"group": g - 1}, {"group": g + 1})

    def fcopy(l, k):
        return pltpu.make_async_remote_copy(
            src_ref=fsrc.at[l, k],
            dst_ref=tab_h.at[l, k],
            send_sem=fs.at[l, k],
            recv_sem=fr.at[l, k],
            device_id=out_dev[k],
            device_id_type=MESH,
        )

    def bcopy(l, k):
        return pltpu.make_async_remote_copy(
            src_ref=bsrc.at[l, k],
            dst_ref=ret.at[l, k],
            send_sem=bs.at[l, k],
            recv_sem=br.at[l, k],
            device_id=in_dev[k],
            device_id_type=MESH,
        )

    def send_halo(l):
        for k in range(4):
            @pl.when(out_ok[k])
            def _(k=k):
                fcopy(l, k).start()

    def wait_halo(l):
        for k in range(4):
            @pl.when(in_ok[k])
            def _(k=k):
                fcopy(l, k).wait_recv()

    def send_ret(l):
        for k in range(4):
            @pl.when(in_ok[k])
            def _(k=k):
                bcopy(l, k).start()

    def wait_ret(l):
        for k in range(4):
            @pl.when(out_ok[k])
            def _(k=k):
                bcopy(l, k).wait_recv()

    far_first = sorted(range(1, D), key=lambda off: abs(2 * off - D))

    def a_copy(t, l, off):
        peer = lax.rem(d + off, D)
        return pltpu.make_async_remote_copy(
            src_ref=grads[t].at[l, peer],
            dst_ref=buf_a[t].at[l, off - 1],
            send_sem=a_s.at[t, l],
            recv_sem=a_r.at[t, l],
            device_id={"dom": peer},
            device_id_type=MESH,
        )

    def b_copy(t, l, off):
        return pltpu.make_async_remote_copy(
            src_ref=buf_b[t].at[l, g],
            dst_ref=buf_b[t].at[l, g],
            send_sem=b_s.at[t, l],
            recv_sem=b_r.at[t, l],
            device_id={"group": lax.rem(g + off, G)},
            device_id_type=MESH,
        )

    def c_copy(t, l, off):
        return pltpu.make_async_remote_copy(
            src_ref=gat[t].at[l, d],
            dst_ref=gat[t].at[l, d],
            send_sem=c_s.at[t, l],
            recv_sem=c_r.at[t, l],
            device_id={"dom": lax.rem(d + off, D)},
            device_id_type=MESH,
        )

    def every(ref, send_sem, recv_sem, axis, here, size):
        return pltpu.make_async_remote_copy(
            src_ref=ref,
            dst_ref=ref,
            send_sem=send_sem,
            recv_sem=recv_sem,
            device_id={axis: lax.rem(here + 1, size)},
            device_id_type=MESH,
        )

    def a_all(t, l):
        return every(buf_a[t].at[l, pl.ds(0, D - 1)], a_s.at[t, l], a_r.at[t, l], "dom", d, D)

    def b_all(t, l):
        return every(buf_b[t].at[l, pl.ds(0, G - 1)], b_s.at[t, l], b_r.at[t, l], "group", g, G)

    def c_all(t, l):
        return every(gat[t].at[l, pl.ds(0, D - 1)], c_s.at[t, l], c_r.at[t, l], "dom", d, D)

    def start_a(t, l, pieces):
        rows = sum(p.shape[0] for p in pieces)
        pad = D * shares[t] - rows
        filler = [jnp.zeros((pad, H), F32)] if pad else []
        whole = jnp.concatenate(list(pieces) + filler, axis=0)
        grads[t][l] = whole.reshape(D, shares[t], H).astype(BF16)
        for off in far_first:
            a_copy(t, l, off).start()

    def start_b(t, l):
        if D > 1:
            a_all(t, l).wait_recv()
        acc = grads[t][l, d].astype(F32)
        for off in range(1, D):
            acc = acc + buf_a[t][l, off - 1].astype(F32)
        buf_b[t][l, g] = acc.astype(BF16)
        for off in range(1, G):
            b_copy(t, l, off).start()

    def start_c(t, l):
        if G > 1:
            b_all(t, l).wait_recv()
        acc = buf_b[t][l, 0].astype(F32)
        for i in range(1, G):
            acc = acc + buf_b[t][l, i].astype(F32)
        gat[t][l, d] = acc.astype(BF16)
        for off in far_first:
            c_copy(t, l, off).start()

    def end_c(t, l):
        if D > 1:
            c_all(t, l).wait_recv()

    barrier = pltpu.get_barrier_semaphore()
    for k in range(4):
        @pl.when(out_ok[k])
        def _(k=k):
            pl.semaphore_signal(barrier, inc=1, device_id=out_dev[k], device_id_type=MESH)

    def count(*flags):
        return sum(jnp.where(flag, 1, 0) for flag in flags)

    steps = [
        (off, [("dom", d, D)] * (off < D - 1) + [("group", g, G)] * (off < G - 1))
        for off in (2**i for i in range(max(D, G).bit_length()))
        if off < max(D, G) - 1
    ]

    def greet(i):
        off, axes = steps[i]
        for axis, here, size in axes:
            @pl.when(here + off < size)
            def _(axis=axis, here=here, off=off):
                pl.semaphore_signal(
                    met.at[i], inc=1, device_id={axis: here + off}, device_id_type=MESH
                )

            @pl.when(here >= off)
            def _(axis=axis, here=here, off=off):
                pl.semaphore_signal(
                    met.at[i], inc=1, device_id={axis: here - off}, device_id_type=MESH
                )

    def greeted(i):
        off, axes = steps[i]
        pl.semaphore_wait(
            met.at[i],
            count(
                *[here + off < size for _, here, size in axes],
                *[here >= off for _, here, _ in axes],
            ),
        )

    def one_hot(row, ref, row0, height, col0):
        width = row.shape[1]
        sub = lax.broadcasted_iota(jnp.int16, (128, width), 0)
        for j in range(height // 128):
            at = (row - 128 * j).astype(jnp.int16)
            ref[row0 + j * 128 : row0 + (j + 1) * 128, col0 : col0 + width] = jnp.where(
                at == sub, BF16(1), BF16(0)
            )

    def spread(row):
        return jnp.broadcast_to(row, (128, row.shape[1])).T

    def one_hot_rows(ids, height, col0):
        lane = lax.broadcasted_iota(jnp.int16, (W, 128), 1)
        for i in range(E // W):
            at = spread(ids[:, i * W : (i + 1) * W]).astype(jnp.int16)
            for j in range(height // 128):
                oh[i * W : (i + 1) * W, col0 + j * 128 : col0 + (j + 1) * 128] = jnp.where(
                    at - jnp.int16(128 * j) == lane, BF16(1), BF16(0)
                )

    def halo_out(l, x_t):
        sent = mm(x_t, o_x[...]).astype(BF16)
        for k in range(4):
            fsrc[l, k] = sent[:, k * HALO : (k + 1) * HALO]

    for k in range(4):
        @pl.when(jnp.logical_not(in_ok[k]))
        def _(k=k):
            for l in range(L):
                tab_h[l, k] = jnp.zeros((H, HALO), BF16)

        @pl.when(jnp.logical_not(out_ok[k]))
        def _(k=k):
            for l in range(L):
                ret[l, k] = jnp.zeros((H, HALO), BF16)

    loads[0].wait()
    loads[1].wait()
    x_t = nodes[0].T
    tab[0] = x_t
    for k in range(4):
        one_hot(sidx[0, k : k + 1, :], o_x, 0, N, k * HALO)
    halo_out(0, x_t)
    pl.semaphore_wait(barrier, count(*out_ok))
    send_halo(0)
    if steps:
        greet(0)

    for load in loads[2:5]:
        load.wait()
    sids = snd[...]
    past = sids - N
    edge_0 = cnt[0, 0]
    edge_1 = edge_0 + cnt[0, 1]
    edge_2 = edge_1 + cnt[0, 2]
    sids = (
        sids
        + jnp.where(past >= edge_0, HALO - cnt[0, 0], 0)
        + jnp.where(past >= edge_1, HALO - cnt[0, 1], 0)
        + jnp.where(past >= edge_2, HALO - cnt[0, 2], 0)
    )
    rids = rcv[...]
    RQ, RS, RH = H, H + N, H + 2 * N
    TOP = RH + 4 * HALO
    one_hot(rids, rhs, RQ, N, 0)
    one_hot(sids, rhs, RS, N + 4 * HALO, 0)

    for load in loads[5:]:
        load.wait()
    first = edges[0].T
    stk[0, :H, :] = first
    rhs[:H, :] = first

    def column(row):
        return jnp.broadcast_to(row, (128, H)).T

    def centred(w, row):
        w = w.astype(F32)
        w = w - jnp.mean(w, axis=1, keepdims=True)
        col = column(row - jnp.mean(row, axis=1, keepdims=True))[:, :16]
        high = col.astype(BF16).astype(F32)
        mid = (col - high).astype(BF16).astype(F32)
        lane = lax.broadcasted_iota(jnp.int32, col.shape, 1)
        split = jnp.where(
            lane == 0,
            high,
            jnp.where(lane == 1, mid, jnp.where(lane == 2, col - high - mid, 0.0)),
        )
        return w.astype(BF16).T, split.astype(BF16)

    for l in range(L):
        for j in range(3):
            w1_t[l, j] = halved(w1[l, j * H : (j + 1) * H, :].T)
        w1_sq[l, :, :H] = w1[l, 2 * H :, :]
        w1_sq[l, :, H:] = w1[l, H : 2 * H, :]
        w2_t[l, :, :H], w2_t[l, :, H:] = centred(w2[l], bias[l, 1:2, :])
        w2_b[l] = halved(w2[l])
        n1_t[l] = halved(n1[l].T)
        n2_t[l, :, :H], n2_t[l, :, H:] = centred(n2[l], bias[l, 3:4, :])
        n2_b[l] = halved(n2[l])
        for j in range(2):
            cols[l, j] = column(bias[l, 2 * j : 2 * j + 1, :] * 0.5)
            cols[l, 2 + j] = column(gain[l, j : j + 1, :])

    def own_part(l):
        x_t = tab[l]
        own_l[:, :H] = w1_t[l, 0]
        own_l[:, H : H + N] = mm(w1_t[l, 2], x_t).astype(BF16)
        own_l[:, H + N :] = mm(w1_t[l, 1], x_t).astype(BF16)
        for i in range(E // W):
            part = slice(i * W, (i + 1) * W)
            slope[l, :, part] = mm(own_l[...], rhs[:RH, part]) + wide(cols[l, 0], W)

    for l in range(L):
        stk[l, H : H + 16, :] = jnp.ones((16, E), BF16)
        hid[l, H:, :] = jnp.ones((16, E), BF16)
        nhid[l, H:, :] = jnp.ones((16, N), BF16)
    one_hot_rows(rids, N, 0)

    def halo_rows(l):
        return jnp.concatenate([tab_h[l, k] for k in range(4)], axis=1)

    for l in range(L):
        own_part(l)
        if l == 0 and len(steps) > 1:
            greeted(0)
            greet(1)
        if l == L - 1:
            if l > 0:
                halos = halo_rows(0)
                stk[0, H + 16 : 2 * H + 16, :] = (
                    mm(tab[0], rhs[RS:RH, :]) + mm(halos, rhs[RH:, :])
                ).astype(BF16)
                stk[0, 2 * H + 16 :, :] = mm(tab[0], rhs[RQ:RS, :]).astype(BF16)
            one_hot_rows(sids, N + 4 * HALO, N)
            for i in range(2, len(steps)):
                greeted(i - 1)
                greet(i)
        wait_halo(l)
        if l == L - 1 and l == 0:
            halos = halo_rows(0)
            stk[0, H + 16 : 2 * H + 16, :] = (
                mm(tab[0], rhs[RS:RH, :]) + mm(halos, rhs[RH:, :])
            ).astype(BF16)
            stk[0, 2 * H + 16 :, :] = mm(tab[0], rhs[RQ:RS, :]).astype(BF16)
        for k in range(4):
            halo_l[:, k * HALO : (k + 1) * HALO] = mm(w1_t[l, 1], tab_h[l, k]).astype(BF16)

        def hidden(i, l=l):
            part = slice(i * W, (i + 1) * W)
            h_b, sl = silu_half(slope[l, :, part] + mm(halo_l[...], rhs[RH:, part]))
            hid[l, :H, part] = h_b
            slope[l, :, part] = sl

        def update(i, l=l):
            part = slice(i * W, (i + 1) * W)
            hat_c, inv_c = norm_parts(mm(w2_t[l], hid[l, :, part]))
            hat[l, :, part] = hat_c
            inv[l, :, part] = inv_c
            new = (stk[l, :H, part].astype(F32) + hat_c * wide(cols[l, 2], W)).astype(BF16)
            if l + 1 < L:
                stk[l + 1, :H, part] = new
                rhs[:H, part] = new
            else:
                e_last[:, part] = new

        for i in range(E // W):
            hidden(i)
        for i in range(E // W):
            update(i)

        x_t = tab[l]
        e_new = stk[l + 1, :H, :] if l + 1 < L else e_last[...]
        joined = jnp.concatenate([x_t, mm(e_new, oh[:, :N]).astype(BF16)], axis=0)
        jn[l] = joined
        h_b, sl = silu_half(mm(n1_t[l], joined) + wide(cols[l, 1], N))
        nhid[l, :H, :] = h_b
        nslope[l] = sl
        hat_c, inv_c = norm_parts(mm(n2_t[l], nhid[l]))
        nhat[l] = hat_c
        ninv[l] = inv_c
        x_new = (x_t.astype(F32) + hat_c * wide(cols[l, 3], N)).astype(BF16)
        if l + 1 < L:
            tab[l + 1] = x_new
            halo_out(l + 1, x_new)
            send_halo(l + 1)
        else:
            x_out[0] = x_new.T

    ones_n = jnp.ones((16, N), BF16)
    for l in reversed(range(L)):
        cot = ncot[0].T.astype(F32) if l == L - 1 else x_cot.astype(F32)
        dmn, nuh = norm_back(cot, wide(cols[l, 3], N), nhat[l], ninv[l])
        dmn = dmn.astype(BF16)
        dpn = (mm(n2_b[l], dmn) * nslope[l]).astype(BF16)
        djn = mm(n1[l], dpn)
        dx[...] = cot + djn[:H, :]
        dab = djn[H:, :].astype(BF16)

        def node_grads(dge, db1, db2, l=l, dpn=dpn, dmn=dmn, nuh=nuh):
            one = mm_nt(jnp.concatenate([jn[l], ones_n], axis=0), dpn)
            two = mm_nt(nhid[l], dmn)
            start_a(
                0,
                l,
                [
                    one[: 2 * H],
                    two[:H],
                    db1,
                    db2,
                    one[2 * H : 2 * H + 1],
                    two[H : H + 1],
                    lane_sum(dge) / gain[l, 0:1, :],
                    lane_sum(fold(nuh)) / gain[l, 1:2, :],
                ],
            )

        dge = jnp.zeros((H, 128), F32)

        def norm_cot(i, dge, l=l, dab=dab):
            part = slice(i * W, (i + 1) * W)
            c = mm(dab, rhs[RQ:RS, part])
            if l < L - 1:
                c = c + de[:, part].astype(F32)
            dm_c, uh_c = norm_back(c, wide(cols[l, 2], W), hat[l, :, part], inv[l, :, part])
            dm[:, part] = dm_c.astype(BF16)
            cc[:, part] = c
            return dge + fold(uh_c)

        def pre_cot(i, l=l):
            part = slice(i * W, (i + 1) * W)
            dp[:, part] = (mm(w2_b[l], dm[:, part]) * slope[l, :, part]).astype(BF16)

        for i in range(E // W):
            dge = norm_cot(i, dge)
        for i in range(E // W):
            pre_cot(i)

        def halo_cots(l=l):
            u_h = mm(dp[...], oh[:, 2 * N :]).astype(BF16)
            for k in range(4):
                bsrc[l, k] = mm(
                    w1[l, H : 2 * H, :], u_h[:, k * HALO : (k + 1) * HALO]
                ).astype(BF16)
            send_ret(l)
            return u_h

        if l > 0:
            u_h = halo_cots()
            for i in range(E // W):
                part = slice(i * W, (i + 1) * W)
                de[:, part] = (cc[:, part] + mm(w1[l, :H, :], dp[:, part])).astype(BF16)
            u_o = mm(dp[...], oh[:, : 2 * N]).astype(BF16)
            one = mm_nt(stk[l, : H + 16, :], dp[...])
            two = mm_nt(hid[l], dm[...])
            w1_rows = [
                one[:H],
                mm_nt(tab[l], u_o[:, N:]) + mm_nt(halo_rows(l), u_h),
                mm_nt(tab[l], u_o[:, :N]),
            ]
            if l + 1 < L:
                start_b(0, l + 1)
                start_b(1, l + 1)
                start_c(0, l + 1)
                start_c(1, l + 1)
        else:
            one = mm_nt(stk[0], dp[...])
            two = mm_nt(hid[0], dm[...])
            start_a(
                1,
                0,
                [one[:H], one[H + 16 :], two[:H]],
            )
            node_grads(dge, one[H : H + 1], two[H : H + 1])
            if L > 1:
                start_b(0, 1)
                start_b(1, 1)
            halo_cots()
            u_o = mm(dp[...], oh[:, : 2 * N]).astype(BF16)
        total = dx[...] + mm(
            w1_sq[l], jnp.concatenate([u_o[:, :N], u_o[:, N:]], axis=0)
        )
        if l > 0:
            if l == L - 1 and steps:
                greeted(len(steps) - 1)
            start_a(
                1,
                l,
                w1_rows + [two[:H]],
            )
            node_grads(dge, one[H : H + 1], two[H : H + 1])
        else:
            for i in range(E // W):
                part = slice(i * W, (i + 1) * W)
                back = (cc[:, part] + mm(w1[l, :H, :], dp[:, part])).astype(BF16)
                e_grad[0, part, :] = back.T
            start_b(1, 0)
            start_b(0, 0)
            if L > 1:
                start_c(0, 1)
                start_c(1, 1)
        wait_ret(l)
        back_in = jnp.concatenate([ret[l, k] for k in range(4)], axis=1)
        x_cot = (total + mm_nt(back_in, o_x[...])).astype(BF16)
    x_grad[0] = x_cot.T

    for l in range(L):
        for k in range(4):
            @pl.when(out_ok[k])
            def _(k=k, l=l):
                fcopy(l, k).wait_send()

            @pl.when(in_ok[k])
            def _(k=k, l=l):
                bcopy(l, k).wait_send()
        for t in range(2):
            if D > 1:
                a_all(t, l).wait_send()
            if l > 0 and G > 1:
                b_all(t, l).wait_send()

    start_c(1, 0)
    start_c(0, 0)
    for t in range(2):
        if G > 1:
            b_all(t, 0).wait_send()
        for l in range(1, L):
            end_c(t, l)
            if D > 1:
                c_all(t, l).wait_send()
    for t in (1, 0):
        end_c(t, 0)
        if D > 1:
            c_all(t, 0).wait_send()


def finish(
    scale, H, x0, xg0, eg0, sum_n, sum_e,
    x1, xg1, eg1, g_w1, g_w2, g_n1, g_n2, g_b, g_g,
    v_w1, v_w2, v_n1, v_n2, v_b, v_g, sem,
):
    copies = [
        pltpu.make_async_copy(src, dst, sem.at[i])
        for i, (src, dst) in enumerate(((eg0, eg1), (x0, x1), (xg0, xg1)))
    ]
    for copy in copies:
        copy.start()
    L, D, share_n, _ = sum_n.shape
    share_e = sum_e.shape[2]
    for l in range(L):
        edge = (sum_e[l].astype(F32) * scale).reshape(D * share_e, H)
        v_w1[l] = edge[: 3 * H]
        v_w2[l] = edge[3 * H : 4 * H]
    copies.append(pltpu.make_async_copy(v_w1, g_w1, sem.at[3]))
    copies[-1].start()
    for l in range(L):
        node = (sum_n[l].astype(F32) * scale).reshape(D * share_n, H)
        v_n1[l] = node[: 2 * H]
        v_n2[l] = node[2 * H : 3 * H]
        node = node[3 * H : 3 * H + 8]
        v_b[l] = node[0:4]
        v_g[l] = node[4:6]
    for i, (src, dst) in enumerate(
        ((v_n1, g_n1), (v_n2, g_n2), (v_w2, g_w2), (v_b, g_b), (v_g, g_g))
    ):
        copies.append(pltpu.make_async_copy(src, dst, sem.at[4 + i]))
        copies[-1].start()
    for copy in copies:
        copy.wait()


def shards(D, G, nodes, edges, node_cot, send_index, halo_count, senders, receivers, *weights):
    edge_in_w, edge_out_w, node_in_w, node_out_w, biases, gains = weights
    _, N, H = nodes.shape
    E = edges.shape[1]
    L = edge_in_w.shape[0]
    HALO = send_index.shape[2]
    W = 256
    share_n = -(-(3 * H + 6) // (8 * D)) * 8
    share_e = -(-4 * H // (8 * D)) * 8
    dims = (D, G, L, N, E, H, HALO, W, share_n, share_e)
    T = N + 4 * HALO
    own_shape = (
        pltpu.VMEM(nodes.shape, BF16),
        pltpu.VMEM(nodes.shape, BF16),
        pltpu.VMEM(edges.shape, BF16),
        pltpu.VMEM((L, D, share_n, H), BF16),
        pltpu.VMEM((L, D, share_e, H), BF16),
    )
    out_shape = (
        jax.ShapeDtypeStruct(nodes.shape, BF16),
        jax.ShapeDtypeStruct(nodes.shape, BF16),
        jax.ShapeDtypeStruct(edges.shape, BF16),
        jax.ShapeDtypeStruct(edge_in_w.shape, F32),
        jax.ShapeDtypeStruct(edge_out_w.shape, F32),
        jax.ShapeDtypeStruct(node_in_w.shape, F32),
        jax.ShapeDtypeStruct(node_out_w.shape, F32),
        jax.ShapeDtypeStruct(biases.shape, F32),
        jax.ShapeDtypeStruct(gains.shape, F32),
    )
    V = pltpu.VMEM
    dma = pltpu.SemaphoreType.DMA
    scratch = [
        V((H + N + T, E), BF16),
        V((N, 4 * HALO), BF16),
        V((H, H + 2 * N), BF16),
        V((H, 4 * HALO), BF16),
        V((L, H, N), BF16),
        V((L, 4, H, HALO), BF16),
        V((E, T + N), BF16),
        V((L, 3 * H + 16, E), BF16),
        V((H, E), BF16),
        V((L, H + 16, E), BF16),
        V((L, H, E), F32),
        V((L, H, E), F32),
        V((L, 1, E), F32),
        V((L, 2 * H, N), BF16),
        V((L, H + 16, N), BF16),
        V((L, H, N), F32),
        V((L, H, N), F32),
        V((L, 1, N), F32),
        V((L, 4, H, 128), F32),
        V((L, 3, H, H), BF16),
        V((L, H, 2 * H), BF16),
        V((L, H, H + 16), BF16),
        V((L, H, H), BF16),
        V((L, H, 2 * H), BF16),
        V((L, H, H + 16), BF16),
        V((L, H, H), BF16),
        V((H, E), BF16),
        V((H, E), BF16),
        V((H, E), F32),
        V((H, E), BF16),
        V((H, N), F32),
        V((L, 4, H, HALO), BF16),
        V((L, 4, H, HALO), BF16),
        V((L, 4, H, HALO), BF16),
        V((L, D, share_n, H), BF16),
        V((L, max(D - 1, 1), share_n, H), BF16),
        V((L, G, share_n, H), BF16),
        V((L, D, share_e, H), BF16),
        V((L, max(D - 1, 1), share_e, H), BF16),
        V((L, G, share_e, H), BF16),
        dma((L, 4)),
        dma((L, 4)),
        dma((L, 4)),
        dma((L, 4)),
        dma((2, L)),
        dma((2, L)),
        dma((2, L)),
        dma((2, L)),
        dma((2, L)),
        dma((2, L)),
        pltpu.SMEM(halo_count.shape, jnp.int32),
    ]
    operands = (nodes, edges, node_cot, send_index, senders, receivers) + weights
    scratch += [V(x.shape, x.dtype) for x in operands] + [dma((13,)), pltpu.SemaphoreType.REGULAR((max(D, G).bit_length(),))]
    vm = pl.BlockSpec(memory_space=pltpu.VMEM)
    hbm = pl.BlockSpec(memory_space=pltpu.HBM)
    own = pl.pallas_call(
        functools.partial(kernel, dims),
        out_shape=own_shape,
        in_specs=[hbm] * 13,
        out_specs=tuple([vm] * 5),
        scratch_shapes=scratch,
        compiler_params=pltpu.CompilerParams(
            collective_id=0, has_side_effects=True, vmem_limit_bytes=VMEM_MAIN
        ),
    )(
        halo_count,
        *operands,
    )
    scale = (D * G * N) ** (-0.5)
    return pl.pallas_call(
        functools.partial(finish, scale, H),
        out_shape=out_shape,
        in_specs=[vm] * 5,
        out_specs=tuple([hbm] * 9),
        scratch_shapes=[V(x.shape, F32) for x in (edge_in_w, edge_out_w, node_in_w, node_out_w)]
        + [V(biases.shape, F32), V(gains.shape, F32), dma((9,))],
        compiler_params=pltpu.CompilerParams(vmem_limit_bytes=8 * 1024 * 1024),
    )(*own)


def solution(mesh):
    part3 = P(("dom", "group"), None, None)
    part2 = P(("dom", "group"), None)
    in_specs = (part3, part3, part3, part3, part2, part2, part2) + (P(),) * 6
    out_specs = (part3, part3, part3) + (P(),) * 6
    body = functools.partial(shards, mesh.shape["dom"], mesh.shape["group"])
    return jax.shard_map(
        body, mesh=mesh, in_specs=in_specs, out_specs=out_specs, check_vma=False
    )
```

```python
import functools

import jax
import jax.numpy as jnp
from jax import lax
from jax.experimental import pallas as pl
from jax.experimental.pallas import tpu as pltpu
from jax.sharding import PartitionSpec as P

F32 = jnp.float32
BF16 = jnp.bfloat16
MESH = pl.DeviceIdType.MESH
VMEM_MAIN = 58 * 1024 * 1024


def mm(a, b):
    return lax.dot_general(a, b, (((1,), (0,)), ((), ())), preferred_element_type=F32)


def mm_nt(a, b):
    return lax.dot_general(a, b, (((1,), (1,)), ((), ())), preferred_element_type=F32)


def norm_parts(values):
    spread = jnp.mean(values * values, axis=0, keepdims=True)
    inv = lax.rsqrt(spread + 1e-05)
    return values * inv, inv


def norm_back(cot, gain_col, hat, inv):
    u = cot * gain_col
    uh = u * hat
    back = inv * (
        u
        - jnp.mean(u, axis=0, keepdims=True)
        - hat * jnp.mean(uh, axis=0, keepdims=True)
    )
    return back, uh


def fold(x):
    total = x[:, :128]
    for i in range(1, x.shape[1] // 128):
        total = total + x[:, i * 128 : (i + 1) * 128]
    return total


def lane_sum(x):
    return jnp.sum(x.T, axis=0, keepdims=True)


def silu_half(half):
    t = jnp.tanh(half)
    a = 1.0 + t
    h = half * a
    return h.astype(BF16), a + h * (1.0 - t)


def halved(x):
    return (x.astype(F32) * 0.5).astype(BF16)


def wide(tile, width):
    return jnp.concatenate([tile] * (width // tile.shape[1]), axis=1)


def kernel(
    dims,
    cnt_h,
    nodes_h,
    edges_h,
    ncot_h,
    sidx_h,
    snd_h,
    rcv_h,
    w1_h,
    w2_h,
    n1_h,
    n2_h,
    bias_h,
    gain_h,
    x_out,
    x_grad,
    e_grad,
    sum_n,
    sum_e,
    rhs,
    o_x,
    own_l,
    halo_l,
    tab,
    tab_h,
    oh,
    stk,
    e_last,
    hid,
    slope,
    hat,
    inv,
    jn,
    nhid,
    nslope,
    nhat,
    ninv,
    cols,
    w1_t,
    w1_sq,
    w2_t,
    w2_b,
    n1_t,
    n2_t,
    n2_b,
    dm,
    dp,
    cc,
    de,
    dx,
    fsrc,
    bsrc,
    ret,
    grads_n,
    buf_an,
    buf_bn,
    grads_e,
    buf_ae,
    buf_be,
    fs,
    fr,
    bs,
    br,
    a_s,
    a_r,
    b_s,
    b_r,
    c_s,
    c_r,
    cnt,
    nodes,
    edges,
    ncot,
    sidx,
    snd,
    rcv,
    w1,
    w2,
    n1,
    n2,
    bias,
    gain,
    in_sem,
    met,
):
    D, G, L, N, E, H, HALO, W, share_n, share_e = dims
    shares = (share_n, share_e)
    grads = (grads_n, grads_e)
    buf_a = (buf_an, buf_ae)
    buf_b = (buf_bn, buf_be)
    gat = (sum_n, sum_e)
    loads = [
        pltpu.make_async_copy(src, dst, in_sem.at[i])
        for i, (src, dst) in enumerate(
            (
                (nodes_h, nodes),
                (sidx_h, sidx),
                (snd_h, snd),
                (rcv_h, rcv),
                (cnt_h, cnt),
                (edges_h, edges),
                (w1_h, w1),
                (w2_h, w2),
                (bias_h, bias),
                (gain_h, gain),
                (n1_h, n1),
                (n2_h, n2),
                (ncot_h, ncot),
            )
        )
    ]
    loads[0].start()
    loads[1].start()
    d = lax.axis_index("dom")
    g = lax.axis_index("group")

    has_up = d + 1 < D
    has_down = d > 0
    has_right = g + 1 < G
    has_left = g > 0
    out_ok = (has_up, has_down, has_right, has_left)
    in_ok = (has_down, has_up, has_left, has_right)
    out_dev = ({"dom": d + 1}, {"dom": d - 1}, {"group": g + 1}, {"group": g - 1})
    in_dev = ({"dom": d - 1}, {"dom": d + 1}, {"group": g - 1}, {"group": g + 1})

    barrier = pltpu.get_barrier_semaphore()
    for k in range(4):
        @pl.when(out_ok[k])
        def _(k=k):
            pl.semaphore_signal(barrier, inc=1, device_id=out_dev[k], device_id_type=MESH)

    for load in loads[2:]:
        load.start()

    def fcopy(l, k):
        return pltpu.make_async_remote_copy(
            src_ref=fsrc.at[l, k],
            dst_ref=tab_h.at[l, k],
            send_sem=fs.at[l, k],
            recv_sem=fr.at[l, k],
            device_id=out_dev[k],
            device_id_type=MESH,
        )

    def bcopy(l, k):
        return pltpu.make_async_remote_copy(
            src_ref=bsrc.at[l, k],
            dst_ref=ret.at[l, k],
            send_sem=bs.at[l, k],
            recv_sem=br.at[l, k],
            device_id=in_dev[k],
            device_id_type=MESH,
        )

    def send_halo(l):
        for k in range(4):
            @pl.when(out_ok[k])
            def _(k=k):
                fcopy(l, k).start()

    def wait_halo(l):
        for k in range(4):
            @pl.when(in_ok[k])
            def _(k=k):
                fcopy(l, k).wait_recv()

    def send_ret(l):
        for k in range(4):
            @pl.when(in_ok[k])
            def _(k=k):
                bcopy(l, k).start()

    def wait_ret(l):
        for k in range(4):
            @pl.when(out_ok[k])
            def _(k=k):
                bcopy(l, k).wait_recv()

    far_first = sorted(range(1, D), key=lambda off: -abs(2 * off - D))

    def a_copy(t, l, off):
        peer = lax.rem(d + off, D)
        return pltpu.make_async_remote_copy(
            src_ref=grads[t].at[l, peer],
            dst_ref=buf_a[t].at[l, off - 1],
            send_sem=a_s.at[t, l],
            recv_sem=a_r.at[t, l],
            device_id={"dom": peer},
            device_id_type=MESH,
        )

    def b_copy(t, l, off):
        return pltpu.make_async_remote_copy(
            src_ref=buf_b[t].at[l, g],
            dst_ref=buf_b[t].at[l, g],
            send_sem=b_s.at[t, l],
            recv_sem=b_r.at[t, l],
            device_id={"group": lax.rem(g + off, G)},
            device_id_type=MESH,
        )

    def c_copy(t, l, off):
        return pltpu.make_async_remote_copy(
            src_ref=gat[t].at[l, d],
            dst_ref=gat[t].at[l, d],
            send_sem=c_s.at[t, l],
            recv_sem=c_r.at[t, l],
            device_id={"dom": lax.rem(d + off, D)},
            device_id_type=MESH,
        )

    def every(ref, send_sem, recv_sem, axis, here, size):
        return pltpu.make_async_remote_copy(
            src_ref=ref,
            dst_ref=ref,
            send_sem=send_sem,
            recv_sem=recv_sem,
            device_id={axis: lax.rem(here + 1, size)},
            device_id_type=MESH,
        )

    def a_all(t, l):
        return every(buf_a[t].at[l, pl.ds(0, D - 1)], a_s.at[t, l], a_r.at[t, l], "dom", d, D)

    def b_all(t, l):
        return every(buf_b[t].at[l, pl.ds(0, G - 1)], b_s.at[t, l], b_r.at[t, l], "group", g, G)

    def c_all(t, l):
        return every(gat[t].at[l, pl.ds(0, D - 1)], c_s.at[t, l], c_r.at[t, l], "dom", d, D)

    def start_a(t, l, pieces):
        rows = sum(p.shape[0] for p in pieces)
        pad = D * shares[t] - rows
        filler = [jnp.zeros((pad, H), F32)] if pad else []
        whole = jnp.concatenate(list(pieces) + filler, axis=0)
        grads[t][l] = whole.reshape(D, shares[t], H).astype(BF16)
        for off in far_first:
            a_copy(t, l, off).start()

    def start_b(t, l):
        if D > 1:
            a_all(t, l).wait_recv()
        acc = grads[t][l, d].astype(F32)
        for off in range(1, D):
            acc = acc + buf_a[t][l, off - 1].astype(F32)
        buf_b[t][l, g] = acc.astype(BF16)
        for off in range(1, G):
            b_copy(t, l, off).start()

    def start_c(t, l):
        if G > 1:
            b_all(t, l).wait_recv()
        acc = buf_b[t][l, 0].astype(F32)
        for i in range(1, G):
            acc = acc + buf_b[t][l, i].astype(F32)
        gat[t][l, d] = acc.astype(BF16)
        for off in far_first:
            c_copy(t, l, off).start()

    def end_c(t, l):
        if D > 1:
            c_all(t, l).wait_recv()

    def count(*flags):
        return sum(jnp.where(flag, 1, 0) for flag in flags)

    steps = [
        (off, [("dom", d, D)] * (off < D - 1) + [("group", g, G)] * (off < G - 1))
        for off in (2**i for i in range(max(D, G).bit_length()))
        if off < max(D, G) - 1
    ]

    def greet(i):
        off, axes = steps[i]
        for axis, here, size in axes:
            @pl.when(here + off < size)
            def _(axis=axis, here=here, off=off):
                pl.semaphore_signal(
                    met.at[i], inc=1, device_id={axis: here + off}, device_id_type=MESH
                )

            @pl.when(here >= off)
            def _(axis=axis, here=here, off=off):
                pl.semaphore_signal(
                    met.at[i], inc=1, device_id={axis: here - off}, device_id_type=MESH
                )

    def greeted(i):
        off, axes = steps[i]
        pl.semaphore_wait(
            met.at[i],
            count(
                *[here + off < size for _, here, size in axes],
                *[here >= off for _, here, _ in axes],
            ),
        )

    def one_hot(row, ref, row0, height, col0):
        width = row.shape[1]
        sub = lax.broadcasted_iota(jnp.int16, (128, width), 0)
        for j in range(height // 128):
            at = (row - 128 * j).astype(jnp.int16)
            ref[row0 + j * 128 : row0 + (j + 1) * 128, col0 : col0 + width] = jnp.where(
                at == sub, BF16(1), BF16(0)
            )

    def spread(row):
        return jnp.broadcast_to(row, (128, row.shape[1])).T

    def one_hot_rows(ids, height, col0):
        lane = lax.broadcasted_iota(jnp.int16, (W, 128), 1)
        for i in range(E // W):
            at = spread(ids[:, i * W : (i + 1) * W]).astype(jnp.int16)
            for j in range(height // 128):
                oh[i * W : (i + 1) * W, col0 + j * 128 : col0 + (j + 1) * 128] = jnp.where(
                    at - jnp.int16(128 * j) == lane, BF16(1), BF16(0)
                )

    def halo_out(l, x_t):
        sent = mm(x_t, o_x[...]).astype(BF16)
        for k in range(4):
            fsrc[l, k] = sent[:, k * HALO : (k + 1) * HALO]

    for k in range(4):
        @pl.when(jnp.logical_not(in_ok[k]))
        def _(k=k):
            for l in range(L):
                tab_h[l, k] = jnp.zeros((H, HALO), BF16)

        @pl.when(jnp.logical_not(out_ok[k]))
        def _(k=k):
            for l in range(L):
                ret[l, k] = jnp.zeros((H, HALO), BF16)

    loads[0].wait()
    loads[1].wait()
    x_t = nodes[0].T
    tab[0] = x_t
    for k in range(4):
        one_hot(sidx[0, k : k + 1, :], o_x, 0, N, k * HALO)
    halo_out(0, x_t)
    pl.semaphore_wait(barrier, count(*out_ok))
    send_halo(0)
    if steps:
        greet(0)

    for load in loads[2:5]:
        load.wait()
    sids = snd[...]
    past = sids - N
    edge_0 = cnt[0, 0]
    edge_1 = edge_0 + cnt[0, 1]
    edge_2 = edge_1 + cnt[0, 2]
    sids = (
        sids
        + jnp.where(past >= edge_0, HALO - cnt[0, 0], 0)
        + jnp.where(past >= edge_1, HALO - cnt[0, 1], 0)
        + jnp.where(past >= edge_2, HALO - cnt[0, 2], 0)
    )
    rids = rcv[...]
    RQ, RS, RH = H, H + N, H + 2 * N
    TOP = RH + 4 * HALO
    one_hot(rids, rhs, RQ, N, 0)
    one_hot(sids, rhs, RS, N + 4 * HALO, 0)

    for load in loads[5:]:
        load.wait()
    first = edges[0].T
    stk[0, :H, :] = first
    rhs[:H, :] = first

    def column(row):
        return jnp.broadcast_to(row, (128, H)).T

    def centred(w, row):
        w = w.astype(F32)
        w = w - jnp.mean(w, axis=1, keepdims=True)
        col = column(row - jnp.mean(row, axis=1, keepdims=True))[:, :16]
        high = col.astype(BF16).astype(F32)
        mid = (col - high).astype(BF16).astype(F32)
        lane = lax.broadcasted_iota(jnp.int32, col.shape, 1)
        split = jnp.where(
            lane == 0,
            high,
            jnp.where(lane == 1, mid, jnp.where(lane == 2, col - high - mid, 0.0)),
        )
        return w.astype(BF16).T, split.astype(BF16)

    for l in range(L):
        for j in range(3):
            w1_t[l, j] = halved(w1[l, j * H : (j + 1) * H, :].T)
        w1_sq[l, :, :H] = w1[l, 2 * H :, :]
        w1_sq[l, :, H:] = w1[l, H : 2 * H, :]
        w2_t[l, :, :H], w2_t[l, :, H:] = centred(w2[l], bias[l, 1:2, :])
        w2_b[l] = halved(w2[l])
        n1_t[l] = halved(n1[l].T)
        n2_t[l, :, :H], n2_t[l, :, H:] = centred(n2[l], bias[l, 3:4, :])
        n2_b[l] = halved(n2[l])
        for j in range(2):
            cols[l, j] = column(bias[l, 2 * j : 2 * j + 1, :] * 0.5)
            cols[l, 2 + j] = column(gain[l, j : j + 1, :])

    def own_part(l):
        x_t = tab[l]
        own_l[:, :H] = w1_t[l, 0]
        own_l[:, H : H + N] = mm(w1_t[l, 2], x_t).astype(BF16)
        own_l[:, H + N :] = mm(w1_t[l, 1], x_t).astype(BF16)
        for i in range(E // W):
            part = slice(i * W, (i + 1) * W)
            slope[l, :, part] = mm(own_l[...], rhs[:RH, part]) + wide(cols[l, 0], W)

    for l in range(L):
        stk[l, H : H + 16, :] = jnp.ones((16, E), BF16)
        hid[l, H:, :] = jnp.ones((16, E), BF16)
        nhid[l, H:, :] = jnp.ones((16, N), BF16)
    one_hot_rows(rids, N, 0)

    def halo_rows(l):
        return jnp.concatenate([tab_h[l, k] for k in range(4)], axis=1)

    for l in range(L):
        own_part(l)
        if l == 0 and len(steps) > 1:
            greeted(0)
            greet(1)
        if l == L - 1:
            if l > 0:
                halos = halo_rows(0)
                stk[0, H + 16 : 2 * H + 16, :] = (
                    mm(tab[0], rhs[RS:RH, :]) + mm(halos, rhs[RH:, :])
                ).astype(BF16)
                stk[0, 2 * H + 16 :, :] = mm(tab[0], rhs[RQ:RS, :]).astype(BF16)
            one_hot_rows(sids, N + 4 * HALO, N)
            for i in range(2, len(steps)):
                greeted(i - 1)
                greet(i)
        wait_halo(l)
        if l == L - 1 and l == 0:
            halos = halo_rows(0)
            stk[0, H + 16 : 2 * H + 16, :] = (
                mm(tab[0], rhs[RS:RH, :]) + mm(halos, rhs[RH:, :])
            ).astype(BF16)
            stk[0, 2 * H + 16 :, :] = mm(tab[0], rhs[RQ:RS, :]).astype(BF16)
        for k in range(4):
            halo_l[:, k * HALO : (k + 1) * HALO] = mm(w1_t[l, 1], tab_h[l, k]).astype(BF16)

        def hidden(i, l=l):
            part = slice(i * W, (i + 1) * W)
            h_b, sl = silu_half(slope[l, :, part] + mm(halo_l[...], rhs[RH:, part]))
            hid[l, :H, part] = h_b
            slope[l, :, part] = sl

        def update(i, l=l):
            part = slice(i * W, (i + 1) * W)
            hat_c, inv_c = norm_parts(mm(w2_t[l], hid[l, :, part]))
            hat[l, :, part] = hat_c
            inv[l, :, part] = inv_c
            new = (stk[l, :H, part].astype(F32) + hat_c * wide(cols[l, 2], W)).astype(BF16)
            if l + 1 < L:
                stk[l + 1, :H, part] = new
                rhs[:H, part] = new
            else:
                e_last[:, part] = new

        for i in range(E // W):
            hidden(i)
        for i in range(E // W):
            update(i)

        x_t = tab[l]
        e_new = stk[l + 1, :H, :] if l + 1 < L else e_last[...]
        joined = jnp.concatenate([x_t, mm(e_new, oh[:, :N]).astype(BF16)], axis=0)
        jn[l] = joined
        h_b, sl = silu_half(mm(n1_t[l], joined) + wide(cols[l, 1], N))
        nhid[l, :H, :] = h_b
        nslope[l] = sl
        hat_c, inv_c = norm_parts(mm(n2_t[l], nhid[l]))
        nhat[l] = hat_c
        ninv[l] = inv_c
        x_new = (x_t.astype(F32) + hat_c * wide(cols[l, 3], N)).astype(BF16)
        if l + 1 < L:
            tab[l + 1] = x_new
            halo_out(l + 1, x_new)
            send_halo(l + 1)
        else:
            x_out[0] = x_new.T

    ones_n = jnp.ones((16, N), BF16)
    for l in reversed(range(L)):
        cot = ncot[0].T.astype(F32) if l == L - 1 else x_cot.astype(F32)
        dmn, nuh = norm_back(cot, wide(cols[l, 3], N), nhat[l], ninv[l])
        dmn = dmn.astype(BF16)
        dpn = (mm(n2_b[l], dmn) * nslope[l]).astype(BF16)
        djn = mm(n1[l], dpn)
        dx[...] = cot + djn[:H, :]
        dab = djn[H:, :].astype(BF16)

        def node_grads(dge, db1, db2, l=l, dpn=dpn, dmn=dmn, nuh=nuh):
            one = mm_nt(jnp.concatenate([jn[l], ones_n], axis=0), dpn)
            two = mm_nt(nhid[l], dmn)
            start_a(
                0,
                l,
                [
                    one[: 2 * H],
                    two[:H],
                    db1,
                    db2,
                    one[2 * H : 2 * H + 1],
                    two[H : H + 1],
                    lane_sum(dge) / gain[l, 0:1, :],
                    lane_sum(fold(nuh)) / gain[l, 1:2, :],
                ],
            )

        dge = jnp.zeros((H, 128), F32)

        def norm_cot(i, dge, l=l, dab=dab):
            part = slice(i * W, (i + 1) * W)
            c = mm(dab, rhs[RQ:RS, part])
            if l < L - 1:
                c = c + de[:, part].astype(F32)
            dm_c, uh_c = norm_back(c, wide(cols[l, 2], W), hat[l, :, part], inv[l, :, part])
            dm[:, part] = dm_c.astype(BF16)
            cc[:, part] = c
            return dge + fold(uh_c)

        def pre_cot(i, l=l):
            part = slice(i * W, (i + 1) * W)
            dp[:, part] = (mm(w2_b[l], dm[:, part]) * slope[l, :, part]).astype(BF16)

        for i in range(E // W):
            dge = norm_cot(i, dge)
        for i in range(E // W):
            pre_cot(i)

        def halo_cots(l=l):
            u_h = mm(dp[...], oh[:, 2 * N :]).astype(BF16)
            for k in range(4):
                bsrc[l, k] = mm(
                    w1[l, H : 2 * H, :], u_h[:, k * HALO : (k + 1) * HALO]
                ).astype(BF16)
            send_ret(l)
            return u_h

        if l > 0:
            u_h = halo_cots()
            u_o = mm(dp[...], oh[:, : 2 * N]).astype(BF16)
            one = mm_nt(stk[l, : H + 16, :], dp[...])
            two = mm_nt(hid[l], dm[...])
            w1_rows = [
                one[:H],
                mm_nt(tab[l], u_o[:, N:]) + mm_nt(halo_rows(l), u_h),
                mm_nt(tab[l], u_o[:, :N]),
            ]
            if l == L - 1 and steps:
                greeted(len(steps) - 1)
            start_a(
                1,
                l,
                w1_rows + [two[:H]],
            )
            node_grads(dge, one[H : H + 1], two[H : H + 1])
            if l + 1 < L:
                start_b(0, l + 1)
                start_b(1, l + 1)
                start_c(0, l + 1)
                start_c(1, l + 1)
        else:
            one = mm_nt(stk[0], dp[...])
            two = mm_nt(hid[0], dm[...])
            start_a(
                1,
                0,
                [one[:H], one[H + 16 :], two[:H]],
            )
            if L > 1:
                start_b(0, 1)
                start_b(1, 1)
            node_grads(dge, one[H : H + 1], two[H : H + 1])
            halo_cots()
            u_o = mm(dp[...], oh[:, : 2 * N]).astype(BF16)
        total = dx[...] + mm(
            w1_sq[l], jnp.concatenate([u_o[:, :N], u_o[:, N:]], axis=0)
        )
        if l > 0:
            for i in range(E // W):
                part = slice(i * W, (i + 1) * W)
                de[:, part] = (cc[:, part] + mm(w1[l, :H, :], dp[:, part])).astype(BF16)
        else:
            for i in range(E // W):
                part = slice(i * W, (i + 1) * W)
                back = (cc[:, part] + mm(w1[l, :H, :], dp[:, part])).astype(BF16)
                e_grad[0, part, :] = back.T
            start_b(1, 0)
            start_b(0, 0)
            if L > 1:
                start_c(0, 1)
                start_c(1, 1)
        if l == 0:
            break
        wait_ret(l)
        back_in = jnp.concatenate([ret[l, k] for k in range(4)], axis=1)
        x_cot = (total + mm_nt(back_in, o_x[...])).astype(BF16)
    for l in range(L):
        for k in range(4):
            @pl.when(out_ok[k])
            def _(k=k, l=l):
                fcopy(l, k).wait_send()

            @pl.when(in_ok[k])
            def _(k=k, l=l):
                bcopy(l, k).wait_send()
        for t in range(2):
            if D > 1:
                a_all(t, l).wait_send()
            if l > 0 and G > 1:
                b_all(t, l).wait_send()

    start_c(1, 0)
    start_c(0, 0)
    wait_ret(0)
    back_in = jnp.concatenate([ret[0, k] for k in range(4)], axis=1)
    x_cot = (total + mm_nt(back_in, o_x[...])).astype(BF16)
    x_grad[0] = x_cot.T
    for t in range(2):
        if G > 1:
            b_all(t, 0).wait_send()
        for l in range(1, L):
            end_c(t, l)
            if D > 1:
                c_all(t, l).wait_send()
    for t in (1, 0):
        end_c(t, 0)
        if D > 1:
            c_all(t, 0).wait_send()


def finish(
    scale, H, x0, xg0, eg0, sum_n, sum_e,
    x1, xg1, eg1, g_w1, g_w2, g_n1, g_n2, g_b, g_g,
    v_w1, v_w2, v_n1, v_n2, v_b, v_g, sem,
):
    copies = [
        pltpu.make_async_copy(src, dst, sem.at[i])
        for i, (src, dst) in enumerate(((eg0, eg1), (x0, x1), (xg0, xg1)))
    ]
    for copy in copies:
        copy.start()
    L, D, share_n, _ = sum_n.shape
    share_e = sum_e.shape[2]
    for l in range(L):
        edge = (sum_e[l].astype(F32) * scale).reshape(D * share_e, H)
        v_w1[l] = edge[: 3 * H]
        v_w2[l] = edge[3 * H : 4 * H]
    copies.append(pltpu.make_async_copy(v_w1, g_w1, sem.at[3]))
    copies[-1].start()
    for l in range(L):
        node = (sum_n[l].astype(F32) * scale).reshape(D * share_n, H)
        v_n1[l] = node[: 2 * H]
        v_n2[l] = node[2 * H : 3 * H]
        node = node[3 * H : 3 * H + 8]
        v_b[l] = node[0:4]
        v_g[l] = node[4:6]
    for i, (src, dst) in enumerate(
        ((v_n1, g_n1), (v_n2, g_n2), (v_w2, g_w2), (v_b, g_b), (v_g, g_g))
    ):
        copies.append(pltpu.make_async_copy(src, dst, sem.at[4 + i]))
        copies[-1].start()
    for copy in copies:
        copy.wait()


def shards(D, G, nodes, edges, node_cot, send_index, halo_count, senders, receivers, *weights):
    edge_in_w, edge_out_w, node_in_w, node_out_w, biases, gains = weights
    _, N, H = nodes.shape
    E = edges.shape[1]
    L = edge_in_w.shape[0]
    HALO = send_index.shape[2]
    W = 256
    share_n = -(-(3 * H + 6) // (8 * D)) * 8
    share_e = -(-4 * H // (8 * D)) * 8
    dims = (D, G, L, N, E, H, HALO, W, share_n, share_e)
    T = N + 4 * HALO
    own_shape = (
        pltpu.VMEM(nodes.shape, BF16),
        pltpu.VMEM(nodes.shape, BF16),
        pltpu.VMEM(edges.shape, BF16),
        pltpu.VMEM((L, D, share_n, H), BF16),
        pltpu.VMEM((L, D, share_e, H), BF16),
    )
    out_shape = (
        jax.ShapeDtypeStruct(nodes.shape, BF16),
        jax.ShapeDtypeStruct(nodes.shape, BF16),
        jax.ShapeDtypeStruct(edges.shape, BF16),
        jax.ShapeDtypeStruct(edge_in_w.shape, F32),
        jax.ShapeDtypeStruct(edge_out_w.shape, F32),
        jax.ShapeDtypeStruct(node_in_w.shape, F32),
        jax.ShapeDtypeStruct(node_out_w.shape, F32),
        jax.ShapeDtypeStruct(biases.shape, F32),
        jax.ShapeDtypeStruct(gains.shape, F32),
    )
    V = pltpu.VMEM
    dma = pltpu.SemaphoreType.DMA
    scratch = [
        V((H + N + T, E), BF16),
        V((N, 4 * HALO), BF16),
        V((H, H + 2 * N), BF16),
        V((H, 4 * HALO), BF16),
        V((L, H, N), BF16),
        V((L, 4, H, HALO), BF16),
        V((E, T + N), BF16),
        V((L, 3 * H + 16, E), BF16),
        V((H, E), BF16),
        V((L, H + 16, E), BF16),
        V((L, H, E), F32),
        V((L, H, E), F32),
        V((L, 1, E), F32),
        V((L, 2 * H, N), BF16),
        V((L, H + 16, N), BF16),
        V((L, H, N), F32),
        V((L, H, N), F32),
        V((L, 1, N), F32),
        V((L, 4, H, 128), F32),
        V((L, 3, H, H), BF16),
        V((L, H, 2 * H), BF16),
        V((L, H, H + 16), BF16),
        V((L, H, H), BF16),
        V((L, H, 2 * H), BF16),
        V((L, H, H + 16), BF16),
        V((L, H, H), BF16),
        V((H, E), BF16),
        V((H, E), BF16),
        V((H, E), F32),
        V((H, E), BF16),
        V((H, N), F32),
        V((L, 4, H, HALO), BF16),
        V((L, 4, H, HALO), BF16),
        V((L, 4, H, HALO), BF16),
        V((L, D, share_n, H), BF16),
        V((L, max(D - 1, 1), share_n, H), BF16),
        V((L, G, share_n, H), BF16),
        V((L, D, share_e, H), BF16),
        V((L, max(D - 1, 1), share_e, H), BF16),
        V((L, G, share_e, H), BF16),
        dma((L, 4)),
        dma((L, 4)),
        dma((L, 4)),
        dma((L, 4)),
        dma((2, L)),
        dma((2, L)),
        dma((2, L)),
        dma((2, L)),
        dma((2, L)),
        dma((2, L)),
        pltpu.SMEM(halo_count.shape, jnp.int32),
    ]
    operands = (nodes, edges, node_cot, send_index, senders, receivers) + weights
    scratch += [V(x.shape, x.dtype) for x in operands] + [dma((13,)), pltpu.SemaphoreType.REGULAR((max(D, G).bit_length(),))]
    vm = pl.BlockSpec(memory_space=pltpu.VMEM)
    hbm = pl.BlockSpec(memory_space=pltpu.HBM)
    own = pl.pallas_call(
        functools.partial(kernel, dims),
        out_shape=own_shape,
        in_specs=[hbm] * 13,
        out_specs=tuple([vm] * 5),
        scratch_shapes=scratch,
        compiler_params=pltpu.CompilerParams(
            collective_id=0, has_side_effects=True, vmem_limit_bytes=VMEM_MAIN
        ),
    )(
        halo_count,
        *operands,
    )
    scale = (D * G * N) ** (-0.5)
    return pl.pallas_call(
        functools.partial(finish, scale, H),
        out_shape=out_shape,
        in_specs=[vm] * 5,
        out_specs=tuple([hbm] * 9),
        scratch_shapes=[V(x.shape, F32) for x in (edge_in_w, edge_out_w, node_in_w, node_out_w)]
        + [V(biases.shape, F32), V(gains.shape, F32), dma((9,))],
        compiler_params=pltpu.CompilerParams(vmem_limit_bytes=8 * 1024 * 1024),
    )(*own)


def solution(mesh):
    part3 = P(("dom", "group"), None, None)
    part2 = P(("dom", "group"), None)
    in_specs = (part3, part3, part3, part3, part2, part2, part2) + (P(),) * 6
    out_specs = (part3, part3, part3) + (P(),) * 6
    body = functools.partial(shards, mesh.shape["dom"], mesh.shape["group"])
    return jax.shard_map(
        body, mesh=mesh, in_specs=in_specs, out_specs=out_specs, check_vma=False
    )
```
